256 devices in a mesh: samp: 16 (over x, y), ind: 16 (over z, core).
Axes of the slice: x: 4, y: 4, z: 8, core: 2. Of those that a mesh axis runs over, the one named last changes fastest.
Arguments:
- points: bfloat16 [32768, 64], P('samp'), may hold values from -6 to 6
- centers: bfloat16 [65536, 64], P('ind'), may hold values from -6 to 6
- coeffs: bfloat16 [65536, 128], P('ind'), may hold values from -0.6 to 0.6
- targets: bfloat16 [32768, 128], P('samp'), may hold values from 0 to 1
- diag_inv: float32 [128, 512, 512], P('ind'), may hold values from -3 to 15
- low_left: bfloat16 [128, 512, 64], P('ind'), may hold values from -0.0014648438 to 0.0014648438
- low_right: bfloat16 [128, 512, 64], P('ind'), may hold values from -0.25 to 0.25
- decay_rates: float32 [128, 64], P('ind'), may hold values from 0.05 to 64
- block_ranks: int32 [128], P('ind'), may hold values from 16 to 64
Outputs:
- direction: float32 [65536, 128], P('ind')
The draws below stay inside these ranges and needn't reach their ends.
All inputs are finite; a program needn't handle non-finite values.
Results may differ from the reference program's by a relative error of at most 0.0003.
Values may be sent and summed in bfloat16 or wider, within the bound.
No kernel may reach another device: no remote copies, remote signals or barrier semaphores. Data moves between devices by JAX's collectives and lax.ppermute only.
A program may use at most 128 MiB of HBM per device.

```python
import math
import jax
import jax.numpy as jnp
from jax import lax

D = 64
L = 128
M = 65536
B = 512
R = 64
N = 32768
NB = 128


def draw_coeffs(key, part):
    uniform_key = jax.random.fold_in(key, 0)
    values = jax.random.uniform(uniform_key, (M, L), jnp.float32, -0.3, 0.3)
    return (values - jnp.mean(values, axis=0, keepdims=True)).astype(jnp.bfloat16)


def draw_diag_inv(key, part):
    diag_key, jitter_key = jax.random.split(key)
    leading = jax.random.uniform(diag_key, (NB, B), jnp.float32, 4.0, 12.0)
    jitter = jnp.clip(jax.random.normal(jitter_key, (NB, B, B), jnp.float32), -3.0, 3.0) * (2.0 / math.sqrt(B))
    return jitter + leading[:, :, None] * jnp.eye(B, dtype=jnp.float32)


def with_ends(array, key, low, high):
    shape = array.shape
    place = [jax.random.randint(jax.random.fold_in(key, axis), (), 0, shape[axis]) for axis in range(len(shape))]
    array = array.at[tuple(place)].set(low)
    longest = shape.index(max(shape))
    place[longest] = (place[longest] + 1) % shape[longest]
    return array.at[tuple(place)].set(high)


def block_levels(key, dims, pieces, smallest, top_value):
    level = 1.0
    for dim, shards_of in pieces:
        steps = jax.random.uniform(jax.random.fold_in(jax.random.fold_in(key, 6), dim), (shards_of,), jnp.float32, smallest / len(pieces), top_value / len(pieces))
        level = level * jnp.repeat(jnp.exp(steps), dims[dim] // shards_of).reshape((-1,) + (1,) * (len(dims) - 1 - dim))
    return level


def scatter_about(rng, extent, spread, limit, shards=(), kind=jnp.bfloat16):
    drawn = jax.random.normal(rng, extent, jnp.float32) * spread
    if len(shards) > 0:
        drawn = block_levels(rng, extent, shards, -0.22, 0.18) * drawn
    return jnp.clip(drawn, min=-limit, max=limit).astype(kind)


def setup_inputs(seed: int = 0) -> dict:
    seeds = jax.random.split(jax.random.key(seed), 10)
    return {
        "points": scatter_about(seeds[0], (N, D), 1.0, 6.0, ((0, 16),)),
        "centers": scatter_about(seeds[1], (M, D), 1.0, 6.0, ((0, 16),)),
        "coeffs": draw_coeffs(jax.random.fold_in(seeds[9], 71), 0),
        "targets": jnp.clip(1.0 * jax.random.uniform(seeds[3], (N, L), jnp.float32) ** block_levels(seeds[3], (N, L), ((0, 16),), -0.2, 0.2), 0.0, 1.0).astype(jnp.bfloat16),
        "diag_inv": draw_diag_inv(jax.random.fold_in(seeds[9], 71), 0),
        "low_left": scatter_about(seeds[5], (NB, B, R), (250000 * R) ** -0.5, 0.0014648438, ((0, 16),)),
        "low_right": scatter_about(seeds[6], (NB, B, R), B ** -0.5, 0.25, ((0, 16),)),
        "decay_rates": jnp.clip(jnp.exp(math.log(64.0) - 7.1546153 * jax.random.uniform(seeds[7], (NB, R), jnp.float32) ** block_levels(seeds[7], (NB, R), ((0, 16),), -0.2, 0.2)), 0.05, 64.0),
        "block_ranks": with_ends(jax.random.randint(seeds[8], (NB,), R // 4, R + 1), jax.random.fold_in(seeds[8], 1), R // 4, R).astype(jnp.int32),
    }


highest = lax.Precision.HIGHEST
ridge_weight = 0.1

def kernel_tile(points, point_sq, center_block):
    center_sq = lax.optimization_barrier(jnp.sum(jnp.square(center_block.astype(jnp.float32)), axis=1))
    cross_term = lax.dot_general(points, center_block, (((1,), (1,)), ((), ())), preferred_element_type=jnp.float32)
    distance = point_sq[:, None] + center_sq[None, :] - 2.0 * cross_term
    return jnp.exp(-(1.0 / D) * distance).astype(jnp.bfloat16)

def solve_step(state, inputs):
    inv_block, left_block, right_block, decay_block, grad_block = inputs
    rhs_block = grad_block - jnp.dot(left_block, state, precision=highest)
    solved = jnp.dot(inv_block, rhs_block, precision=highest)
    state = decay_block[:, None] * state + jnp.dot(right_block.T, solved, precision=highest)
    return (state, solved)

def reference(points, centers, coeffs, targets, diag_inv, low_left, low_right, decay_rates, block_ranks):
    block_width = M // 16
    block_count = M // block_width
    point_sq = lax.optimization_barrier(jnp.sum(jnp.square(points.astype(jnp.float32)), axis=1))
    center_blocks = centers.reshape(block_count, block_width, D)
    coeff_blocks = coeffs.reshape(block_count, block_width, L)

    def add_block(running, paired):
        kernel_part = kernel_tile(points, point_sq, paired[0])
        return (running + jnp.dot(kernel_part, paired[1], preferred_element_type=jnp.float32), None)
    prediction, _ = lax.scan(add_block, jnp.zeros((N, L), jnp.float32), (center_blocks, coeff_blocks))
    residual = (jax.nn.sigmoid(prediction) - targets.astype(jnp.float32)).astype(jnp.bfloat16)

    def grad_piece(center_block):
        kernel_part = kernel_tile(points, point_sq, center_block)
        return lax.dot_general(kernel_part, residual, (((0,), (0,)), ((), ())), preferred_element_type=jnp.float32)
    summed = lax.map(grad_piece, center_blocks).reshape(M, L)
    gradient = summed * (1.0 / math.sqrt(N)) + ridge_weight * coeffs.astype(jnp.float32)
    rank_mask = (jnp.arange(R)[None, :] < block_ranks[:, None]).astype(jnp.float32)
    left_masked = low_left.astype(jnp.float32) * rank_mask[:, None, :]
    right_masked = low_right.astype(jnp.float32) * rank_mask[:, None, :]
    decays = jnp.exp(-decay_rates / NB)
    grad_blocks = gradient.reshape(NB, B, L)
    _, solved = lax.scan(solve_step, jnp.zeros((R, L), jnp.float32), (diag_inv, left_masked, right_masked, decays, grad_blocks))
    return solved.reshape(M, L)
```

```python
import functools
import math

import jax
import jax.numpy as jnp
from jax import lax
from jax.experimental import pallas as pl
from jax.experimental.pallas import tpu as pltpu
from jax.sharding import PartitionSpec as P

D = 64
B = 512
R = 64
NB = 128
LOG2E = math.log2(math.e)

f32 = jnp.float32
bf16 = jnp.bfloat16
wire = jnp.float16
ridge_weight = 0.1
highest = lax.Precision.HIGHEST


def dot(a, b, ca, cb):
    return lax.dot_general(a, b, (((ca,), (cb,)), ((), ())), preferred_element_type=f32)


def split(a):
    high = a.astype(bf16)
    return high, (a - high.astype(f32)).astype(bf16)


def dot3(a, b, ca, cb):
    ah, al = split(a)
    bh, bl = split(b)
    return dot(ah, bh, ca, cb) + (dot(ah, bl, ca, cb) + dot(al, bh, ca, cb))


def predict_kernel(width, points_t, centers_t, coeffs, kernel_out, pred):
    x_t = points_t[...].astype(f32)
    x32 = x_t.T
    x = x32.astype(bf16)
    p = jnp.sum(x32 * x32, axis=1, keepdims=True) * (-LOG2E / D)
    total = None
    for at in range(0, centers_t.shape[1], width):
        c = centers_t[:, at : at + width]
        c32 = c.astype(f32)
        q = jnp.sum(c32 * c32, axis=0, keepdims=True) * (-LOG2E / D)
        exponent = dot(x, c, 1, 0) * (2 * LOG2E / D) + (p + q)
        k = jnp.exp2(exponent).astype(bf16)
        kernel_out[:, at : at + width] = k
        part = dot(k, coeffs[at : at + width, :], 1, 0)
        total = part if total is None else total + part
    pred[...] = total


def predict(points_t, centers_t, coeffs, rows=512, width=256):
    n, m, labels = points_t.shape[1], centers_t.shape[1], coeffs.shape[1]
    return pl.pallas_call(
        functools.partial(predict_kernel, width),
        grid=(n // rows,),
        in_specs=[
            pl.BlockSpec((D, rows), lambda i: (0, i)),
            pl.BlockSpec((D, m), lambda i: (0, 0)),
            pl.BlockSpec((m, labels), lambda i: (0, 0)),
        ],
        out_specs=[
            pl.BlockSpec((rows, m), lambda i: (i, 0)),
            pl.BlockSpec((rows, labels), lambda i: (i, 0)),
        ],
        out_shape=[
            jax.ShapeDtypeStruct((n, m), bf16),
            jax.ShapeDtypeStruct((n, labels), f32),
        ],
        compiler_params=pltpu.CompilerParams(vmem_limit_bytes=40 << 20),
        cost_estimate=pl.CostEstimate(
            flops=2 * n * m * (D + labels), bytes_accessed=2 * n * m, transcendentals=n * m
        ),
        name="predict",
    )(points_t, centers_t, coeffs)


def gradient_kernel(residual, kernel_cols, out, turned):
    @pl.when(pl.program_id(0) == 0)
    def _():
        turned[...] = residual[...].astype(f32).T.astype(bf16)

    out[...] = dot(turned[...], kernel_cols[...], 1, 0)


def gradient_t(residual, stored, cols=1024):
    n, labels = residual.shape
    m = stored.shape[1]
    return pl.pallas_call(
        gradient_kernel,
        grid=(m // cols,),
        in_specs=[
            pl.BlockSpec((n, labels), lambda i: (0, 0)),
            pl.BlockSpec((n, cols), lambda i: (0, i)),
        ],
        out_specs=pl.BlockSpec((labels, cols), lambda i: (0, i)),
        out_shape=jax.ShapeDtypeStruct((labels, m), f32),
        scratch_shapes=[pltpu.VMEM((labels, n), bf16)],
        compiler_params=pltpu.CompilerParams(vmem_limit_bytes=40 << 20),
        cost_estimate=pl.CostEstimate(
            flops=2 * n * m * labels, bytes_accessed=2 * n * m, transcendentals=0
        ),
        name="gradient",
    )(residual, stored)


def prepare_kernel(ranks, inverse, left_t, right_t, rates, proj, step, side, suffix_proj, transfer, acc):
    i = pl.program_id(0)
    k = pl.num_programs(0) - 1 - i
    eye = lax.broadcasted_iota(jnp.int32, (R, R), 0) == lax.broadcasted_iota(jnp.int32, (R, R), 1)

    @pl.when(i == 0)
    def _():
        acc[...] = eye.astype(f32)

    kept = lax.broadcasted_iota(jnp.int32, (R, B), 0) < ranks[k]
    left = jnp.where(kept, left_t[0].astype(f32), 0.0).astype(bf16)
    right = jnp.where(kept, right_t[0].astype(f32), 0.0).astype(bf16)
    high, low = split(inverse[0])
    p = dot(right, high, 1, 0) + dot(right, low, 1, 0)
    proj[...] = p
    side[...] = dot(left, high, 1, 1) + dot(left, low, 1, 1)
    ph, plow = split(p)
    decay = jnp.exp(rates[0] * (-1.0 / NB))
    a = jnp.where(eye, decay, 0.0) - (dot(ph, left, 1, 1) + dot(plow, left, 1, 1))
    step[0] = a
    suffix = acc[...]
    suffix_proj[...] = dot3(suffix, p, 1, 0)
    suffix = jnp.dot(suffix, a, precision=highest, preferred_element_type=f32)
    acc[...] = suffix
    transfer[...] = jnp.concatenate([suffix, jnp.zeros_like(suffix)], axis=1)


def prepare(block_ranks, diag_inv, left_t, right_t, rates):
    count = diag_inv.shape[0]
    back = lambda i, ranks: (count - 1 - i, 0, 0)
    wide = lambda i, ranks: (0, count - 1 - i)
    wide_shape = jax.ShapeDtypeStruct((R, count * B), f32)
    return pl.pallas_call(
        prepare_kernel,
        grid_spec=pltpu.PrefetchScalarGridSpec(
            num_scalar_prefetch=1,
            grid=(count,),
            in_specs=[
                pl.BlockSpec((1, B, B), back),
                pl.BlockSpec((1, R, B), back),
                pl.BlockSpec((1, R, B), back),
                pl.BlockSpec((1, 1, R), back),
            ],
            out_specs=[
                pl.BlockSpec((R, B), wide),
                pl.BlockSpec((1, R, R), back),
                pl.BlockSpec((R, B), wide),
                pl.BlockSpec((R, B), wide),
                pl.BlockSpec((R, 2 * R), lambda i, ranks: (0, 0)),
            ],
            scratch_shapes=[pltpu.VMEM((R, R), f32)],
        ),
        out_shape=[
            wide_shape,
            jax.ShapeDtypeStruct((count, R, R), f32),
            wide_shape,
            wide_shape,
            jax.ShapeDtypeStruct((R, 2 * R), f32),
        ],
        cost_estimate=pl.CostEstimate(
            flops=8 * count * R * B * B, bytes_accessed=6 * count * B * B, transcendentals=0
        ),
        name="prepare",
    )(block_ranks, diag_inv, left_t, right_t, rates[:, None, :])


def offset_kernel(grad, suffix_proj, out):
    found = dot3(grad[...], suffix_proj[...], 1, 1)
    out[...] = jnp.concatenate([found, jnp.zeros_like(found)], axis=1)


def offset_of(grad, suffix_proj):
    return pl.pallas_call(
        offset_kernel,
        out_shape=jax.ShapeDtypeStruct((grad.shape[0], 2 * R), f32),
        name="offset",
    )(grad, suffix_proj)


def local_kernel(grad, inverse, proj, solved, pushed):
    g = grad[...]
    gh = g.astype(bf16).astype(f32)
    gl = g - gh
    pair = jnp.concatenate([gh, gl]).astype(bf16)
    n = g.shape[0]

    def times(matrix):
        high, low = split(matrix)
        main = dot(pair, high, 1, 1)
        return (main[:n] + main[n:]) + dot(pair, low, 1, 1)[:n]

    solved[...] = times(inverse[0])
    pushed[0] = times(proj[...])


def local_solve(grad, diag_inv, proj):
    count = diag_inv.shape[0]
    labels = grad.shape[0]
    return pl.pallas_call(
        local_kernel,
        grid=(count,),
        in_specs=[
            pl.BlockSpec((labels, B), lambda i: (0, i)),
            pl.BlockSpec((1, B, B), lambda i: (i, 0, 0)),
            pl.BlockSpec((R, B), lambda i: (0, i)),
        ],
        out_specs=[
            pl.BlockSpec((labels, B), lambda i: (0, i)),
            pl.BlockSpec((1, labels, R), lambda i: (i, 0, 0)),
        ],
        out_shape=[
            jax.ShapeDtypeStruct((labels, count * B), f32),
            jax.ShapeDtypeStruct((count, labels, R), f32),
        ],
        cost_estimate=pl.CostEstimate(
            flops=6 * count * labels * B * B, bytes_accessed=4 * count * B * B, transcendentals=0
        ),
        name="local_solve",
    )(grad, diag_inv, proj)


def finish_kernel(entering, step, pushed, side, solved, out):
    state = entering[...]
    for k in range(step.shape[0]):
        cols = slice(k * B, (k + 1) * B)
        out[:, cols] = solved[:, cols] - dot3(state, side[:, cols], 1, 0)
        moved = lax.dot_general(
            state,
            step[k],
            (((1,), (1,)), ((), ())),
            precision=highest,
            preferred_element_type=f32,
        )
        state = moved + pushed[k]


def finish(entering, step, pushed, side, solved):
    return pl.pallas_call(
        finish_kernel,
        out_shape=jax.ShapeDtypeStruct(solved.shape, f32),
        name="finish",
    )(entering, step, pushed, side, solved)


def compose(earlier, latter):
    return (
        jnp.einsum("eij,ejk->eik", latter[0], earlier[0], precision=highest),
        jnp.einsum("elj,eij->eli", earlier[1], latter[0], precision=highest) + latter[1],
    )


def entering_state(transfers, offsets):
    count = transfers.shape[0]
    passed = (jnp.arange(count) < lax.axis_index("ind"))[:, None, None]
    pieces = (
        jnp.where(passed, transfers, jnp.eye(R, dtype=f32)),
        jnp.where(passed, offsets, 0.0),
    )
    while pieces[0].shape[0] > 1:
        pieces = compose(tuple(a[0::2] for a in pieces), tuple(a[1::2] for a in pieces))
    return pieces[1][0]


def sent_to_all(array, axis):
    copies = jnp.broadcast_to(array, (lax.axis_size(axis), *array.shape))
    return lax.all_to_all(copies, axis, split_axis=0, concat_axis=0, tiled=True)


def body(points, centers, coeffs, targets, diag_inv, low_left, low_right, decay_rates, block_ranks):
    n, labels = targets.shape
    m = centers.shape[0]
    ind, samp = lax.axis_size("ind"), lax.axis_size("samp")

    stored, pred = predict(points.T, centers.T, coeffs)
    arrived = lax.all_to_all(
        pred.astype(wire).reshape(ind, n // ind, labels), "ind", 0, 0, tiled=True
    )
    proj, step, side, suffix_proj, transfer = prepare(
        block_ranks,
        diag_inv,
        jnp.swapaxes(low_left, 1, 2),
        jnp.swapaxes(low_right, 1, 2),
        decay_rates,
    )
    pred_own = arrived.astype(f32).sum(axis=0)
    own_targets = lax.dynamic_slice_in_dim(targets, lax.axis_index("ind") * (n // ind), n // ind, 0)
    resid = (jax.nn.sigmoid(pred_own) - own_targets.astype(f32)).astype(bf16)
    residual = lax.all_gather(resid, "ind", axis=0, tiled=True)
    transfers = sent_to_all(transfer, "ind")[:, :, :R]

    partial = gradient_t(residual, stored)
    own = labels // samp
    arrived = lax.all_to_all(partial.astype(wire).reshape(samp, own, m), "samp", 0, 0, tiled=True)
    own_coeffs = lax.dynamic_slice_in_dim(coeffs, lax.axis_index("samp") * own, own, 1).T
    scaling = 1.0 / math.sqrt(n * samp)
    grad = arrived.astype(f32).sum(axis=0) * scaling + ridge_weight * own_coeffs.astype(f32)

    offsets = sent_to_all(offset_of(grad, suffix_proj), "ind")[:, :, :R]
    solved, pushed = local_solve(grad, diag_inv, proj)
    entering = entering_state(transfers, offsets)
    direction = finish(entering, step, pushed, side, solved)
    return sent_to_all(direction, "samp").reshape(labels, m).T


def solution(mesh):
    placed = (
        P("samp", None),
        P("ind", None),
        P("ind", None),
        P("samp", None),
        P("ind", None, None),
        P("ind", None, None),
        P("ind", None, None),
        P("ind", None),
        P("ind"),
    )
    return jax.shard_map(
        body, mesh=mesh, in_specs=placed, out_specs=P("ind", None), check_vma=False
    )
```

```python
import functools
import math

import jax
import jax.numpy as jnp
from jax import lax
from jax.experimental import pallas as pl
from jax.experimental.pallas import tpu as pltpu
from jax.sharding import Mesh
from jax.sharding import PartitionSpec as P

D = 64
B = 512
R = 64
NB = 128
LOG2E = math.log2(math.e)

f32 = jnp.float32
bf16 = jnp.bfloat16
wire = jnp.float16
ridge_weight = 0.1
highest = lax.Precision.HIGHEST


def dot(a, b, ca, cb):
    return lax.dot_general(a, b, (((ca,), (cb,)), ((), ())), preferred_element_type=f32)


def split(a):
    high = a.astype(bf16)
    return high, (a - high.astype(f32)).astype(bf16)


def dot3(a, b, ca, cb):
    ah, al = split(a)
    bh, bl = split(b)
    return dot(ah, bh, ca, cb) + (dot(ah, bl, ca, cb) + dot(al, bh, ca, cb))


def predict_kernel(width, half, points_t, centers_t, coeffs, kernel_out, pred):
    x_t = points_t[...].astype(f32)
    x32 = x_t.T
    x = x32.astype(bf16)
    p = jnp.sum(x32 * x32, axis=1, keepdims=True) * (-LOG2E / D)
    total = None
    for at in range(0, centers_t.shape[1], width):
        c = centers_t[:, at : at + width]
        c32 = c.astype(f32)
        q = jnp.sum(c32 * c32, axis=0, keepdims=True) * (-LOG2E / D)
        exponent = dot(x, c, 1, 0) * (2 * LOG2E / D) + (p + q)
        k = jnp.exp2(exponent).astype(bf16)
        kernel_out[:, at : at + width] = k
        part = dot(k, coeffs[at : at + width, :], 1, 0)
        total = part if total is None else total + part
    pred[...] = total


def predict(half, points_t, centers_t, coeffs, rows=512, width=256):
    n, m, labels = points_t.shape[1] // 2, centers_t.shape[1], coeffs.shape[1]
    steps = n // rows
    return pl.pallas_call(
        functools.partial(predict_kernel, width),
        grid_spec=pltpu.PrefetchScalarGridSpec(
            num_scalar_prefetch=1,
            grid=(steps,),
            in_specs=[
                pl.BlockSpec((D, rows), lambda i, half: (0, half[0] * steps + i)),
                pl.BlockSpec((D, m), lambda i, half: (0, 0)),
                pl.BlockSpec((m, labels), lambda i, half: (0, 0)),
            ],
            out_specs=[
                pl.BlockSpec((rows, m), lambda i, half: (i, 0)),
                pl.BlockSpec((rows, labels), lambda i, half: (i, 0)),
            ],
        ),
        out_shape=[
            jax.ShapeDtypeStruct((n, m), bf16),
            jax.ShapeDtypeStruct((n, labels), f32),
        ],
        compiler_params=pltpu.CompilerParams(vmem_limit_bytes=60 << 20),
        cost_estimate=pl.CostEstimate(
            flops=2 * n * m * (D + labels), bytes_accessed=2 * n * m, transcendentals=n * m
        ),
        name="predict",
    )(half.reshape(1), points_t, centers_t, coeffs)


def gradient_kernel(resid_a, resid_b, rows_a, rows_b, out, turned_a, turned_b):
    @pl.when(pl.program_id(0) == 0)
    def _():
        turned_a[...] = resid_a[...].astype(f32).T.astype(bf16)
        turned_b[...] = resid_b[...].astype(f32).T.astype(bf16)

    out[...] = dot(turned_a[...], rows_a[...], 1, 0) + dot(turned_b[...], rows_b[...], 1, 0)


def gradient_t(resid_a, resid_b, stored_a, stored_b, cols=1024):
    n, labels = resid_a.shape
    m = stored_a.shape[1]
    whole = pl.BlockSpec((n, labels), lambda i: (0, 0))
    part = pl.BlockSpec((n, cols), lambda i: (0, i))
    return pl.pallas_call(
        gradient_kernel,
        grid=(m // cols,),
        in_specs=[whole, whole, part, part],
        out_specs=pl.BlockSpec((labels, cols), lambda i: (0, i)),
        out_shape=jax.ShapeDtypeStruct((labels, m), f32),
        scratch_shapes=[pltpu.VMEM((labels, n), bf16)] * 2,
        compiler_params=pltpu.CompilerParams(vmem_limit_bytes=60 << 20),
        cost_estimate=pl.CostEstimate(
            flops=4 * n * m * labels, bytes_accessed=4 * n * m, transcendentals=0
        ),
        name="gradient",
    )(resid_a, resid_b, stored_a, stored_b)


def prepare_kernel(ranks, inverse, left_t, right_t, rates, proj, step, side, suffix_proj, transfer, acc):
    i = pl.program_id(0)
    k = pl.num_programs(0) - 1 - i
    eye = lax.broadcasted_iota(jnp.int32, (R, R), 0) == lax.broadcasted_iota(jnp.int32, (R, R), 1)

    @pl.when(i == 0)
    def _():
        acc[...] = eye.astype(f32)

    kept = lax.broadcasted_iota(jnp.int32, (R, B), 0) < ranks[k]
    left = jnp.where(kept, left_t[0].astype(f32), 0.0).astype(bf16)
    right = jnp.where(kept, right_t[0].astype(f32), 0.0).astype(bf16)
    high, low = split(inverse[0])
    p = dot(right, high, 1, 0) + dot(right, low, 1, 0)
    proj[...] = p
    side[...] = dot(left, high, 1, 1) + dot(left, low, 1, 1)
    ph, plow = split(p)
    decay = jnp.exp(rates[0] * (-1.0 / NB))
    a = jnp.where(eye, decay, 0.0) - (dot(ph, left, 1, 1) + dot(plow, left, 1, 1))
    step[0] = a
    suffix = acc[...]
    suffix_proj[...] = dot3(suffix, p, 1, 0)
    suffix = jnp.dot(suffix, a, precision=highest, preferred_element_type=f32)
    acc[...] = suffix
    transfer[...] = suffix


def prepare(block_ranks, diag_inv, left_t, right_t, rates):
    count = diag_inv.shape[0]
    back = lambda i, ranks: (count - 1 - i, 0, 0)
    wide = lambda i, ranks: (0, count - 1 - i)
    wide_shape = jax.ShapeDtypeStruct((R, count * B), f32)
    return pl.pallas_call(
        prepare_kernel,
        grid_spec=pltpu.PrefetchScalarGridSpec(
            num_scalar_prefetch=1,
            grid=(count,),
            in_specs=[
                pl.BlockSpec((1, B, B), back),
                pl.BlockSpec((1, R, B), back),
                pl.BlockSpec((1, R, B), back),
                pl.BlockSpec((1, 1, R), back),
            ],
            out_specs=[
                pl.BlockSpec((R, B), wide),
                pl.BlockSpec((1, R, R), back),
                pl.BlockSpec((R, B), wide),
                pl.BlockSpec((R, B), wide),
                pl.BlockSpec((R, R), lambda i, ranks: (0, 0)),
            ],
            scratch_shapes=[pltpu.VMEM((R, R), f32)],
        ),
        out_shape=[
            wide_shape,
            jax.ShapeDtypeStruct((count, R, R), f32),
            wide_shape,
            wide_shape,
            jax.ShapeDtypeStruct((R, R), f32),
        ],
        cost_estimate=pl.CostEstimate(
            flops=8 * count * R * B * B, bytes_accessed=6 * count * B * B, transcendentals=0
        ),
        name="prepare",
    )(block_ranks, diag_inv, left_t, right_t, rates[:, None, :])


def prefix_kernel(step, side, out):
    moved = None
    for k in range(step.shape[0]):
        cols = slice(k * B, (k + 1) * B)
        if moved is None:
            out[:, cols] = side[:, cols]
            moved = step[k].T
        else:
            out[:, cols] = dot3(moved, side[:, cols], 1, 0)
            if k + 1 < step.shape[0]:
                moved = dot3(moved, step[k], 1, 1)


def prefix_side(step, side):
    return pl.pallas_call(
        prefix_kernel,
        out_shape=jax.ShapeDtypeStruct(side.shape, f32),
        cost_estimate=pl.CostEstimate(
            flops=6 * R * side.size, bytes_accessed=8 * side.size, transcendentals=0
        ),
        name="prefix",
    )(step, side)


def offset_kernel(grad, suffix_proj, transfer, out):
    found = dot3(grad[...], suffix_proj[...], 1, 1)
    high = found.astype(bf16).astype(f32)
    t = transfer[...]
    rows = jnp.concatenate(
        [
            jnp.concatenate([t[: R // 2], t[R // 2 :]], axis=1),
            jnp.concatenate([high, found - high], axis=1),
            jnp.zeros((8, 2 * R), f32),
        ]
    ).astype(bf16)
    for e in range(out.shape[0]):
        out[e] = rows


def offset_messages(grad, suffix_proj, transfer, count):
    return pl.pallas_call(
        offset_kernel,
        out_shape=jax.ShapeDtypeStruct((count, R // 2 + 16, 2 * R), bf16),
        name="offset",
    )(grad, suffix_proj, transfer)


def local_kernel(grad, inverse, proj, step, side, solved, state):
    @pl.when(pl.program_id(0) == 0)
    def _():
        state[...] = jnp.zeros_like(state)

    g = grad[...]
    gh = g.astype(bf16).astype(f32)
    pair = jnp.concatenate([gh, g - gh]).astype(bf16)
    n = g.shape[0]

    def times(matrix):
        high, low = split(matrix)
        main = dot(pair, high, 1, 1)
        return (main[:n] + main[n:]) + dot(pair, low, 1, 1)[:n]

    entered = state[...]
    solved[...] = times(inverse[0]) - dot3(entered, side[...], 1, 0)
    state[...] = dot3(entered, step[0], 1, 1) + times(proj[...])


def local_solve(grad, diag_inv, proj, step, side):
    count = diag_inv.shape[0]
    labels = grad.shape[0]
    return pl.pallas_call(
        local_kernel,
        grid=(count,),
        in_specs=[
            pl.BlockSpec((labels, B), lambda i: (0, i)),
            pl.BlockSpec((1, B, B), lambda i: (i, 0, 0)),
            pl.BlockSpec((R, B), lambda i: (0, i)),
            pl.BlockSpec((1, R, R), lambda i: (i, 0, 0)),
            pl.BlockSpec((R, B), lambda i: (0, i)),
        ],
        out_specs=pl.BlockSpec((labels, B), lambda i: (0, i)),
        out_shape=jax.ShapeDtypeStruct((labels, count * B), f32),
        scratch_shapes=[pltpu.VMEM((labels, R), f32)],
        cost_estimate=pl.CostEstimate(
            flops=6 * count * labels * B * B, bytes_accessed=4 * count * B * B, transcendentals=0
        ),
        name="local_solve",
    )(grad, diag_inv, proj, step, side)


def finish_kernel(place, messages, solved, side, out):
    mine = place[0]
    count = messages.shape[0]
    half = R // 2

    def read(e):
        got = messages[e].astype(f32)
        transfer = jnp.concatenate([got[:half, :R], got[:half, R:]]).astype(bf16)
        rows = got[half : half + 8]
        return transfer, rows[:, :R] + rows[:, R:]

    def apply(rows, transfer):
        high, low = split(rows)
        return dot(high, transfer, 1, 1) + dot(low, transfer, 1, 1)

    eye = lax.broadcasted_iota(jnp.int32, (R, R), 0) == lax.broadcasted_iota(jnp.int32, (R, R), 1)
    early = jnp.zeros((8, R), f32)
    late = jnp.concatenate([early, eye.astype(f32)])
    blank = jnp.zeros((R, R), f32)
    for e in range(count // 2):
        transfer, rows = read(e)
        early = jnp.where(e < mine, apply(early, transfer) + rows, early)
        f = e + count // 2
        transfer, rows = read(f)
        moved = apply(late, transfer) + jnp.concatenate([rows, blank])
        late = jnp.where(f < mine, moved, late)
    entering = late[:8] + dot3(early, late[8:], 1, 0)
    z = solved[...] - dot3(entering, side[...], 1, 0)
    top = jnp.max(jnp.abs(z), axis=1, keepdims=True)
    power = jnp.ceil(jnp.log2(jnp.maximum(top, 1e-30)))
    width = z.shape[1]
    out[:, :width] = z * jnp.exp2(-power)
    out[:, width:] = jnp.broadcast_to(power, (8, 2 * R))


def finish(place, messages, solved, side):
    labels, m = solved.shape
    vmem = pl.BlockSpec(memory_space=pltpu.VMEM)
    return pl.pallas_call(
        finish_kernel,
        grid_spec=pltpu.PrefetchScalarGridSpec(
            num_scalar_prefetch=1,
            grid=(),
            in_specs=[vmem, vmem, vmem],
            out_specs=vmem,
        ),
        out_shape=jax.ShapeDtypeStruct((labels, m + 2 * R), f32),
        name="finish",
    )(place.reshape(1), messages, solved, side)


def unscaled_kernel(powers, scaled, out):
    out[...] = (scaled[...] * jnp.exp2(powers[:, :1])).T


def unscaled(whole, cols=1024):
    labels = whole.shape[0]
    m = whole.shape[1] - 2 * R
    return pl.pallas_call(
        unscaled_kernel,
        grid=(m // cols,),
        in_specs=[
            pl.BlockSpec((labels, 2 * R), lambda i: (0, m // (2 * R))),
            pl.BlockSpec((labels, cols), lambda i: (0, i)),
        ],
        out_specs=pl.BlockSpec((cols, labels), lambda i: (i, 0)),
        out_shape=jax.ShapeDtypeStruct((m, labels), f32),
        name="unscaled",
    )(whole, whole)


def sent_to_all(array, axis):
    copies = jnp.broadcast_to(array, (lax.axis_size(axis), *array.shape))
    return lax.all_to_all(copies, axis, split_axis=0, concat_axis=0, tiled=True)


def to_partner(array):
    return lax.ppermute(array, "c", [(0, 1), (1, 0)])


def body(points, centers, coeffs, targets, diag_inv, low_left, low_right, decay_rates, block_ranks):
    n, labels = targets.shape
    m = centers.shape[0]
    chips, samp = lax.axis_size("z"), lax.axis_size("samp")
    chip, core = lax.axis_index("z"), lax.axis_index("c")
    place = chip * 2 + core
    share = n // (2 * chips)

    points_t, centers_t = points.T, centers.T
    stored_b, pred_b = predict(1 - core, points_t, centers_t, coeffs)
    from_partner = to_partner(pred_b)
    stored_a, pred_a = predict(core, points_t, centers_t, coeffs)
    pair_sum = (pred_a + from_partner).astype(wire).reshape(chips, share, labels)
    arrived = lax.all_to_all(pair_sum, "z", 0, 0, tiled=True)
    proj, step, side, suffix_proj, transfer = prepare(
        block_ranks,
        diag_inv,
        jnp.swapaxes(low_left, 1, 2),
        jnp.swapaxes(low_right, 1, 2),
        decay_rates,
    )
    arrived, transfer = lax.optimization_barrier((arrived, transfer))
    pred_own = arrived.astype(f32).sum(axis=0)
    first = core * (n // 2) + chip * share
    own_targets = lax.dynamic_slice_in_dim(targets, first, share, 0)
    resid = (jax.nn.sigmoid(pred_own) - own_targets.astype(f32)).astype(bf16)
    resid_a = sent_to_all(resid, "z").reshape(n // 2, labels)
    resid_b = to_partner(resid_a)

    partial = gradient_t(resid_a, resid_b, stored_a, stored_b)
    own = labels // samp
    sent = partial.astype(wire).reshape(samp, own, m)
    sent, step_late, side_late = lax.optimization_barrier((sent, step, side))
    arrived = lax.all_to_all(sent, "samp", 0, 0, tiled=True)
    side_prefix = prefix_side(step_late, side_late)
    arrived, side_prefix = lax.optimization_barrier((arrived, side_prefix))
    own_coeffs = lax.dynamic_slice_in_dim(coeffs, lax.axis_index("samp") * own, own, 1).T
    scaling = 1.0 / math.sqrt(n * samp)
    grad = arrived.astype(f32).sum(axis=0) * scaling + ridge_weight * own_coeffs.astype(f32)

    messages = offset_messages(grad, suffix_proj, transfer, 2 * chips)
    messages = lax.all_to_all(messages, ("z", "c"), 0, 0, tiled=True)
    solved = local_solve(grad, diag_inv, proj, step, side)
    direction = finish(place, messages, solved, side_prefix)
    whole = sent_to_all(direction.astype(wire), "samp").reshape(labels, m + 2 * R)
    return unscaled(whole.astype(f32))


def solution(mesh):
    finer = Mesh(mesh.devices.reshape(mesh.shape["samp"], -1, 2), ("samp", "z", "c"))
    ind = ("z", "c")
    placed = (
        P("samp", None),
        P(ind, None),
        P(ind, None),
        P("samp", None),
        P(ind, None, None),
        P(ind, None, None),
        P(ind, None, None),
        P(ind, None),
        P(ind),
    )
    return jax.shard_map(
        body, mesh=finer, in_specs=placed, out_specs=P(ind, None), check_vma=False
    )
```

```python
import functools
import math

import jax
import jax.numpy as jnp
from jax import lax
from jax.experimental import pallas as pl
from jax.experimental.pallas import tpu as pltpu
from jax.sharding import Mesh
from jax.sharding import PartitionSpec as P

D = 64
B = 512
R = 64
NB = 128
LOG2E = math.log2(math.e)

f32 = jnp.float32
bf16 = jnp.bfloat16
wire = jnp.float16
ridge_weight = 0.1
highest = lax.Precision.HIGHEST


def dot(a, b, ca, cb):
    return lax.dot_general(a, b, (((ca,), (cb,)), ((), ())), preferred_element_type=f32)


def split(a):
    high = a.astype(bf16)
    return high, (a - high.astype(f32)).astype(bf16)


def dot3(a, b, ca, cb):
    ah, al = split(a)
    bh, bl = split(b)
    return dot(ah, bh, ca, cb) + (dot(ah, bl, ca, cb) + dot(al, bh, ca, cb))


def predict_kernel(width, half, points_t, centers_t, coeffs, kernel_out, pred):
    x_t = points_t[...].astype(f32)
    x32 = x_t.T
    x = x32.astype(bf16)
    p = jnp.sum(x32 * x32, axis=1, keepdims=True) * (-LOG2E / D)
    total = None
    for at in range(0, centers_t.shape[1], width):
        c = centers_t[:, at : at + width]
        c32 = c.astype(f32)
        q = jnp.sum(c32 * c32, axis=0, keepdims=True) * (-LOG2E / D)
        exponent = dot(x, c, 1, 0) * (2 * LOG2E / D) + (p + q)
        k = jnp.exp2(exponent).astype(bf16)
        kernel_out[:, at : at + width] = k
        part = dot(k, coeffs[at : at + width, :], 1, 0)
        total = part if total is None else total + part
    pred[...] = total


def predict(half, points_t, centers_t, coeffs, rows=256, width=256):
    n, m, labels = points_t.shape[1] // 2, centers_t.shape[1], coeffs.shape[1]
    steps = n // rows
    return pl.pallas_call(
        functools.partial(predict_kernel, width),
        grid_spec=pltpu.PrefetchScalarGridSpec(
            num_scalar_prefetch=1,
            grid=(steps,),
            in_specs=[
                pl.BlockSpec((D, rows), lambda i, half: (0, half[0] * steps + i)),
                pl.BlockSpec((D, m), lambda i, half: (0, 0)),
                pl.BlockSpec((m, labels), lambda i, half: (0, 0)),
            ],
            out_specs=[
                pl.BlockSpec((rows, m), lambda i, half: (i, 0)),
                pl.BlockSpec((rows, labels), lambda i, half: (i, 0)),
            ],
        ),
        out_shape=[
            jax.ShapeDtypeStruct((n, m), bf16),
            jax.ShapeDtypeStruct((n, labels), f32),
        ],
        compiler_params=pltpu.CompilerParams(vmem_limit_bytes=60 << 20),
        cost_estimate=pl.CostEstimate(
            flops=2 * n * m * (D + labels), bytes_accessed=2 * n * m, transcendentals=n * m
        ),
        name="predict",
    )(half.reshape(1), points_t, centers_t, coeffs)


def gradient_kernel(resid_a, resid_b, rows_a, rows_b, out, turned_a, turned_b):
    @pl.when(pl.program_id(0) == 0)
    def _():
        turned_a[...] = resid_a[...].astype(f32).T.astype(bf16)
        turned_b[...] = resid_b[...].astype(f32).T.astype(bf16)

    out[...] = dot(turned_a[...], rows_a[...], 1, 0) + dot(turned_b[...], rows_b[...], 1, 0)


def gradient_t(resid_a, resid_b, stored_a, stored_b, cols=1024):
    n, labels = resid_a.shape
    m = stored_a.shape[1]
    whole = pl.BlockSpec((n, labels), lambda i: (0, 0))
    part = pl.BlockSpec((n, cols), lambda i: (0, i))
    return pl.pallas_call(
        gradient_kernel,
        grid=(m // cols,),
        in_specs=[whole, whole, part, part],
        out_specs=pl.BlockSpec((labels, cols), lambda i: (0, i)),
        out_shape=jax.ShapeDtypeStruct((labels, m), f32),
        scratch_shapes=[pltpu.VMEM((labels, n), bf16)] * 2,
        compiler_params=pltpu.CompilerParams(vmem_limit_bytes=56 << 20),
        cost_estimate=pl.CostEstimate(
            flops=4 * n * m * labels, bytes_accessed=4 * n * m, transcendentals=0
        ),
        name="gradient",
    )(resid_a, resid_b, stored_a, stored_b)


def prepare_kernel(last, ranks, inverse, left_t, right_t, rates, *refs):
    proj, step, side, suffix_proj, transfer, acc = refs[-6:]
    i = pl.program_id(0)
    eye = lax.broadcasted_iota(jnp.int32, (R, R), 0) == lax.broadcasted_iota(jnp.int32, (R, R), 1)

    @pl.when(i == 0)
    def _():
        acc[...] = eye.astype(f32) if len(refs) == 6 else refs[0][...]

    kept = lax.broadcasted_iota(jnp.int32, (R, B), 0) < ranks[last - i]
    left = jnp.where(kept, left_t[0].astype(f32), 0.0).astype(bf16)
    right = jnp.where(kept, right_t[0].astype(f32), 0.0).astype(bf16)
    high, low = split(inverse[0])
    p = dot(right, high, 1, 0) + dot(right, low, 1, 0)
    proj[...] = p
    side[...] = dot(left, high, 1, 1) + dot(left, low, 1, 1)
    ph, plow = split(p)
    decay = jnp.exp(rates[0] * (-1.0 / NB))
    a = jnp.where(eye, decay, 0.0) - (dot(ph, left, 1, 1) + dot(plow, left, 1, 1))
    step[0] = a
    suffix = acc[...]
    suffix_proj[...] = dot3(suffix, p, 1, 0)
    suffix = jnp.dot(suffix, a, precision=highest, preferred_element_type=f32)
    acc[...] = suffix
    transfer[...] = suffix


def prepare(block_ranks, diag_inv, left_t, right_t, rates, earlier=None):
    count = diag_inv.shape[0]
    steps = count // 2
    last = count - 1 if earlier is None else steps - 1
    back = lambda i, ranks: (last - i, 0, 0)
    wide = lambda i, ranks: (0, last - i)
    square = pl.BlockSpec((R, R), lambda i, ranks: (0, 0))
    wide_shape = jax.ShapeDtypeStruct((R, count * B), f32)
    kept = () if earlier is None else (earlier[4], *earlier[:4])
    return pl.pallas_call(
        functools.partial(prepare_kernel, last),
        grid_spec=pltpu.PrefetchScalarGridSpec(
            num_scalar_prefetch=1,
            grid=(steps,),
            in_specs=[
                pl.BlockSpec((1, B, B), back),
                pl.BlockSpec((1, R, B), back),
                pl.BlockSpec((1, R, B), back),
                pl.BlockSpec((1, 1, R), back),
            ]
            + ([square] + [pl.BlockSpec(memory_space=pl.ANY)] * 4 if kept else []),
            out_specs=[
                pl.BlockSpec((R, B), wide),
                pl.BlockSpec((1, R, R), back),
                pl.BlockSpec((R, B), wide),
                pl.BlockSpec((R, B), wide),
                square,
            ],
            scratch_shapes=[pltpu.VMEM((R, R), f32)],
        ),
        out_shape=[
            wide_shape,
            jax.ShapeDtypeStruct((count, R, R), f32),
            wide_shape,
            wide_shape,
            jax.ShapeDtypeStruct((R, R), f32),
        ],
        input_output_aliases={6: 0, 7: 1, 8: 2, 9: 3} if kept else {},
        cost_estimate=pl.CostEstimate(
            flops=8 * steps * R * B * B, bytes_accessed=6 * steps * B * B, transcendentals=0
        ),
        compiler_params=pltpu.CompilerParams(vmem_limit_bytes=58 << 20),
        name="prepare",
    )(block_ranks, diag_inv, left_t, right_t, rates[:, None, :], *kept)


def prefix_kernel(step, side, out):
    moved = None
    for k in range(step.shape[0]):
        cols = slice(k * B, (k + 1) * B)
        if moved is None:
            out[:, cols] = side[:, cols]
            moved = step[k].T
        else:
            out[:, cols] = dot3(moved, side[:, cols], 1, 0)
            if k + 1 < step.shape[0]:
                moved = dot3(moved, step[k], 1, 1)


def prefix_side(step, side):
    return pl.pallas_call(
        prefix_kernel,
        out_shape=jax.ShapeDtypeStruct(side.shape, f32),
        cost_estimate=pl.CostEstimate(
            flops=6 * R * side.size, bytes_accessed=8 * side.size, transcendentals=0
        ),
        compiler_params=pltpu.CompilerParams(vmem_limit_bytes=40 << 20),
        name="prefix",
    )(step, side)


def offset_kernel(grad, suffix_proj, transfer, out):
    found = dot3(grad[...], suffix_proj[...], 1, 1)
    high = found.astype(bf16).astype(f32)
    t = transfer[...]
    rows = jnp.concatenate(
        [
            jnp.concatenate([t[: R // 2], t[R // 2 :]], axis=1),
            jnp.concatenate([high, found - high], axis=1),
            jnp.zeros((8, 2 * R), f32),
        ]
    ).astype(bf16)
    for e in range(out.shape[0]):
        out[e] = rows


def offset_messages(grad, suffix_proj, transfer, count):
    return pl.pallas_call(
        offset_kernel,
        out_shape=jax.ShapeDtypeStruct((count, R // 2 + 16, 2 * R), bf16),
        compiler_params=pltpu.CompilerParams(vmem_limit_bytes=40 << 20),
        name="offset",
    )(grad, suffix_proj, transfer)


def local_kernel(grad, inverse, proj, step, side, solved, state):
    @pl.when(pl.program_id(0) == 0)
    def _():
        state[...] = jnp.zeros_like(state)

    g = grad[...]
    gh = g.astype(bf16).astype(f32)
    pair = jnp.concatenate([gh, g - gh]).astype(bf16)
    n = g.shape[0]

    def times(matrix):
        high, low = split(matrix)
        main = dot(pair, high, 1, 1)
        return (main[:n] + main[n:]) + dot(pair, low, 1, 1)[:n]

    entered = state[...]
    solved[...] = times(inverse[0]) - dot3(entered, side[...], 1, 0)
    state[...] = dot3(entered, step[0], 1, 1) + times(proj[...])


def local_solve(grad, diag_inv, proj, step, side):
    count = diag_inv.shape[0]
    labels = grad.shape[0]
    return pl.pallas_call(
        local_kernel,
        grid=(count,),
        in_specs=[
            pl.BlockSpec((labels, B), lambda i: (0, i)),
            pl.BlockSpec((1, B, B), lambda i: (i, 0, 0)),
            pl.BlockSpec((R, B), lambda i: (0, i)),
            pl.BlockSpec((1, R, R), lambda i: (i, 0, 0)),
            pl.BlockSpec((R, B), lambda i: (0, i)),
        ],
        out_specs=pl.BlockSpec((labels, B), lambda i: (0, i)),
        out_shape=jax.ShapeDtypeStruct((labels, count * B), f32),
        scratch_shapes=[pltpu.VMEM((labels, R), f32)],
        cost_estimate=pl.CostEstimate(
            flops=6 * count * labels * B * B, bytes_accessed=4 * count * B * B, transcendentals=0
        ),
        compiler_params=pltpu.CompilerParams(vmem_limit_bytes=56 << 20),
        name="local_solve",
    )(grad, diag_inv, proj, step, side)


def finish_kernel(place, messages, solved, side, out):
    mine = place[0]
    count = messages.shape[0]
    half = R // 2

    def read(e):
        got = messages[e].astype(f32)
        transfer = jnp.concatenate([got[:half, :R], got[:half, R:]]).astype(bf16)
        rows = got[half : half + 8]
        return transfer, rows[:, :R] + rows[:, R:]

    def apply(rows, transfer):
        high, low = split(rows)
        return dot(high, transfer, 1, 1) + dot(low, transfer, 1, 1)

    eye = lax.broadcasted_iota(jnp.int32, (R, R), 0) == lax.broadcasted_iota(jnp.int32, (R, R), 1)
    early = jnp.zeros((8, R), f32)
    late = jnp.concatenate([early, eye.astype(f32)])
    blank = jnp.zeros((R, R), f32)
    for e in range(count // 2):
        transfer, rows = read(e)
        early = jnp.where(e < mine, apply(early, transfer) + rows, early)
        f = e + count // 2
        transfer, rows = read(f)
        moved = apply(late, transfer) + jnp.concatenate([rows, blank])
        late = jnp.where(f < mine, moved, late)
    entering = late[:8] + dot3(early, late[8:], 1, 0)
    z = solved[...] - dot3(entering, side[...], 1, 0)
    top = jnp.max(jnp.abs(z), axis=1, keepdims=True)
    power = jnp.ceil(jnp.log2(jnp.maximum(top, 1e-30)))
    width = z.shape[1]
    out[:, :width] = z * jnp.exp2(-power)
    out[:, width:] = jnp.broadcast_to(power, (8, 2 * R))


def finish(place, messages, solved, side):
    labels, m = solved.shape
    vmem = pl.BlockSpec(memory_space=pltpu.VMEM)
    return pl.pallas_call(
        finish_kernel,
        grid_spec=pltpu.PrefetchScalarGridSpec(
            num_scalar_prefetch=1,
            grid=(),
            in_specs=[vmem, vmem, vmem],
            out_specs=vmem,
        ),
        out_shape=jax.ShapeDtypeStruct((labels, m + 2 * R), f32),
        compiler_params=pltpu.CompilerParams(vmem_limit_bytes=40 << 20),
        name="finish",
    )(place.reshape(1), messages, solved, side)


def unscaled_kernel(powers, scaled, out):
    out[...] = (scaled[...] * jnp.exp2(powers[:, :1])).T


def unscaled(whole, cols=1024):
    labels = whole.shape[0]
    m = whole.shape[1] - 2 * R
    return pl.pallas_call(
        unscaled_kernel,
        grid=(m // cols,),
        in_specs=[
            pl.BlockSpec((labels, 2 * R), lambda i: (0, m // (2 * R))),
            pl.BlockSpec((labels, cols), lambda i: (0, i)),
        ],
        out_specs=pl.BlockSpec((cols, labels), lambda i: (i, 0)),
        out_shape=jax.ShapeDtypeStruct((m, labels), f32),
        compiler_params=pltpu.CompilerParams(vmem_limit_bytes=40 << 20),
        name="unscaled",
    )(whole, whole)


def sent_to_all(array, axis):
    copies = jnp.broadcast_to(array, (lax.axis_size(axis), *array.shape))
    return lax.all_to_all(copies, axis, split_axis=0, concat_axis=0, tiled=True)


def to_partner(array):
    return lax.ppermute(array, "c", [(0, 1), (1, 0)])


def body(points, centers, coeffs, targets, diag_inv, low_left, low_right, decay_rates, block_ranks):
    n, labels = targets.shape
    m = centers.shape[0]
    chips, samp = lax.axis_size("z"), lax.axis_size("samp")
    chip, core = lax.axis_index("z"), lax.axis_index("c")
    place = chip * 2 + core
    share = n // (2 * chips)

    points_t, centers_t = points.T, centers.T
    stored_b, pred_b = predict(1 - core, points_t, centers_t, coeffs)
    from_partner = to_partner(pred_b)
    stored_a, pred_a = predict(core, points_t, centers_t, coeffs)
    pair_sum = (pred_a + from_partner).astype(wire).reshape(chips, share, labels)
    arrived = lax.all_to_all(pair_sum, "z", 0, 0, tiled=True)
    factors = (
        block_ranks,
        diag_inv,
        jnp.swapaxes(low_left, 1, 2),
        jnp.swapaxes(low_right, 1, 2),
        decay_rates,
    )
    halfway = prepare(*factors)
    arrived, halfway = lax.optimization_barrier((arrived, halfway))
    pred_own = arrived.astype(f32).sum(axis=0)
    first = core * (n // 2) + chip * share
    own_targets = lax.dynamic_slice_in_dim(targets, first, share, 0)
    resid = (jax.nn.sigmoid(pred_own) - own_targets.astype(f32)).astype(bf16)
    resid, halfway = lax.optimization_barrier((resid, halfway))
    resid_a = sent_to_all(resid, "z").reshape(n // 2, labels)
    prepared = prepare(*factors, halfway)
    resid_a, prepared = lax.optimization_barrier((resid_a, prepared))
    proj, step, side, suffix_proj, transfer = prepared
    resid_b = to_partner(resid_a)

    partial = gradient_t(resid_a, resid_b, stored_a, stored_b)
    own = labels // samp
    sent = partial.astype(wire).reshape(samp, own, m)
    sent, step_late, side_late = lax.optimization_barrier((sent, step, side))
    arrived = lax.all_to_all(sent, "samp", 0, 0, tiled=True)
    side_prefix = prefix_side(step_late, side_late)
    arrived, side_prefix = lax.optimization_barrier((arrived, side_prefix))
    own_coeffs = lax.dynamic_slice_in_dim(coeffs, lax.axis_index("samp") * own, own, 1).T
    scaling = 1.0 / math.sqrt(n * samp)
    grad = arrived.astype(f32).sum(axis=0) * scaling + ridge_weight * own_coeffs.astype(f32)

    messages = offset_messages(grad, suffix_proj, transfer, 2 * chips)
    messages = lax.all_to_all(messages, ("z", "c"), 0, 0, tiled=True)
    solved = local_solve(grad, diag_inv, proj, step, side)
    direction = finish(place, messages, solved, side_prefix)
    whole = sent_to_all(direction.astype(wire), "samp").reshape(labels, m + 2 * R)
    return unscaled(whole.astype(f32))


def solution(mesh):
    finer = Mesh(mesh.devices.reshape(mesh.shape["samp"], -1, 2), ("samp", "z", "c"))
    ind = ("z", "c")
    placed = (
        P("samp", None),
        P(ind, None),
        P(ind, None),
        P("samp", None),
        P(ind, None, None),
        P(ind, None, None),
        P(ind, None, None),
        P(ind, None),
        P(ind),
    )
    return jax.shard_map(
        body, mesh=finer, in_specs=placed, out_specs=P(ind, None), check_vma=False
    )
```

```python
import functools
import math

import jax
import jax.numpy as jnp
from jax import lax
from jax.experimental import pallas as pl
from jax.experimental.pallas import tpu as pltpu
from jax.sharding import Mesh
from jax.sharding import PartitionSpec as P

D = 64
B = 512
R = 64
NB = 128
LOG2E = math.log2(math.e)

f32 = jnp.float32
bf16 = jnp.bfloat16
wire = jnp.float16
ridge_weight = 0.1
highest = lax.Precision.HIGHEST


def dot(a, b, ca, cb):
    return lax.dot_general(a, b, (((ca,), (cb,)), ((), ())), preferred_element_type=f32)


def split(a):
    high = a.astype(bf16)
    return high, (a - high.astype(f32)).astype(bf16)


def dot3(a, b, ca, cb):
    ah, al = split(a)
    bh, bl = split(b)
    return dot(ah, bh, ca, cb) + (dot(ah, bl, ca, cb) + dot(al, bh, ca, cb))


def with_norms(columns, left):
    half = jnp.sum(columns * columns, axis=0, keepdims=True) * -0.5
    high = half.astype(bf16).astype(f32)
    rest = half - high
    middle = rest.astype(bf16).astype(f32)
    n = columns.shape[1]
    ones = [jnp.ones((1, n), f32)] * 3
    parts = [high, middle, rest - middle]
    extra = parts + ones if left else ones + parts
    return jnp.concatenate([columns, *extra, jnp.zeros((2, n), f32)])


def predict_kernel(width, half, points_t, centers, coeffs, stored, pred, *kept):
    i = pl.program_id(0)
    rows = pred.shape[0]
    if kept:
        centers_t, (centers, coeffs_v) = centers, kept

        @pl.when(i == 0)
        def _():
            centers[...] = with_norms(centers_t[...].astype(f32), False).astype(bf16)
            coeffs_v[...] = coeffs[...]

    x = with_norms(points_t[...].astype(f32), True).T.astype(bf16)
    here = pl.ds(pl.multiple_of(i * rows, rows), rows)
    total = None
    for at in range(0, centers.shape[1], width):
        scaled = dot(x, centers[:, at : at + width], 1, 0) * (2 * LOG2E / D)
        k = jnp.exp2(scaled).astype(bf16)
        stored[here, at : at + width] = k
        part = dot(k, coeffs[at : at + width, :], 1, 0)
        total = part if total is None else total + part
    pred[...] = total


vmem = pl.BlockSpec(memory_space=pltpu.VMEM)


def predict(half, points_t, centers, coeffs, first, rows=512, width=256):
    n, m, labels = points_t.shape[1] // 2, centers.shape[1], coeffs.shape[1]
    steps = n // rows
    whole = lambda i, half: (0, 0)
    outs = [pltpu.VMEM((n, m), bf16), jax.ShapeDtypeStruct((n, labels), f32)]
    if first:
        outs += [pltpu.VMEM((D + 8, m), bf16), pltpu.VMEM((m, labels), bf16)]
    return pl.pallas_call(
        functools.partial(predict_kernel, width),
        grid_spec=pltpu.PrefetchScalarGridSpec(
            num_scalar_prefetch=1,
            grid=(steps,),
            in_specs=[pl.BlockSpec((D, rows), lambda i, half: (0, half[0] * steps + i))]
            + (
                [pl.BlockSpec((D, m), whole), pl.BlockSpec((m, labels), whole)]
                if first
                else [vmem, vmem]
            ),
            out_specs=[vmem, pl.BlockSpec((rows, labels), lambda i, half: (i, 0))]
            + ([vmem, vmem] if first else []),
        ),
        out_shape=outs,
        compiler_params=pltpu.CompilerParams(vmem_limit_bytes=20 << 20),
        cost_estimate=pl.CostEstimate(
            flops=2 * n * m * (D + labels), bytes_accessed=2 * n * m, transcendentals=n * m
        ),
        name="predict",
    )(half.reshape(1), points_t, centers, coeffs)


def gradient_kernel(resid_a, resid_b, rows_a, rows_b, out, turned_a, turned_b):
    i = pl.program_id(0)

    @pl.when(i == 0)
    def _():
        turned_a[...] = resid_a[...].astype(f32).T.astype(bf16)
        turned_b[...] = resid_b[...].astype(f32).T.astype(bf16)

    cols = out.shape[1] // pl.num_programs(0)
    here = pl.ds(pl.multiple_of(i * cols, cols), cols)
    out[:, here] = dot(turned_a[...], rows_a[:, here], 1, 0) + dot(
        turned_b[...], rows_b[:, here], 1, 0
    )


def gradient_t(resid_a, resid_b, stored_a, stored_b, cols=1024):
    n, labels = resid_a.shape
    m = stored_a.shape[1]
    return pl.pallas_call(
        gradient_kernel,
        grid=(m // cols,),
        in_specs=[vmem, vmem, vmem, vmem],
        out_specs=vmem,
        out_shape=pltpu.VMEM((labels, m), f32),
        scratch_shapes=[pltpu.VMEM((labels, n), bf16)] * 2,
        compiler_params=pltpu.CompilerParams(vmem_limit_bytes=16 << 20),
        cost_estimate=pl.CostEstimate(
            flops=4 * n * m * labels, bytes_accessed=4 * n * m, transcendentals=0
        ),
        name="gradient",
    )(resid_a, resid_b, stored_a, stored_b)


def prepare_kernel(last, ranks, inverse, left_t, right_t, rates, *refs):
    proj, step, side, suffix_proj, transfer, acc = refs[-6:]
    i = pl.program_id(0)
    eye = lax.broadcasted_iota(jnp.int32, (R, R), 0) == lax.broadcasted_iota(jnp.int32, (R, R), 1)

    @pl.when(i == 0)
    def _():
        acc[...] = eye.astype(f32) if len(refs) == 6 else refs[0][...]

    kept = lax.broadcasted_iota(jnp.int32, (R, B), 0) < ranks[last - i]
    left = jnp.where(kept, left_t[0].astype(f32), 0.0).astype(bf16)
    right = jnp.where(kept, right_t[0].astype(f32), 0.0).astype(bf16)
    high, low = split(inverse[0])
    p = dot(right, high, 1, 0) + dot(right, low, 1, 0)
    proj[...] = p
    side[...] = dot(left, high, 1, 1) + dot(left, low, 1, 1)
    ph, plow = split(p)
    decay = jnp.exp(rates[0] * (-1.0 / NB))
    a = jnp.where(eye, decay, 0.0) - (dot(ph, left, 1, 1) + dot(plow, left, 1, 1))
    step[0] = a
    suffix = acc[...]
    suffix_proj[...] = dot3(suffix, p, 1, 0)
    suffix = jnp.dot(suffix, a, precision=highest, preferred_element_type=f32)
    acc[...] = suffix
    transfer[...] = suffix


def prepare(block_ranks, diag_inv, left_t, right_t, rates, earlier=None):
    count = diag_inv.shape[0]
    steps = count
    last = count - 1
    back = lambda i, ranks: (last - i, 0, 0)
    wide = lambda i, ranks: (0, last - i)
    square = pl.BlockSpec((R, R), lambda i, ranks: (0, 0))
    wide_shape = jax.ShapeDtypeStruct((R, count * B), f32)
    kept = () if earlier is None else (earlier[4], *earlier[:4])
    return pl.pallas_call(
        functools.partial(prepare_kernel, last),
        grid_spec=pltpu.PrefetchScalarGridSpec(
            num_scalar_prefetch=1,
            grid=(steps,),
            in_specs=[
                pl.BlockSpec((1, B, B), back),
                pl.BlockSpec((1, R, B), back),
                pl.BlockSpec((1, R, B), back),
                pl.BlockSpec((1, 1, R), back),
            ]
            + ([square] + [pl.BlockSpec(memory_space=pl.ANY)] * 4 if kept else []),
            out_specs=[
                pl.BlockSpec((R, B), wide),
                pl.BlockSpec((1, R, R), back),
                pl.BlockSpec((R, B), wide),
                pl.BlockSpec((R, B), wide),
                square,
            ],
            scratch_shapes=[pltpu.VMEM((R, R), f32)],
        ),
        out_shape=[
            wide_shape,
            jax.ShapeDtypeStruct((count, R, R), f32),
            wide_shape,
            wide_shape,
            jax.ShapeDtypeStruct((R, R), f32),
        ],
        input_output_aliases={6: 0, 7: 1, 8: 2, 9: 3} if kept else {},
        cost_estimate=pl.CostEstimate(
            flops=8 * steps * R * B * B, bytes_accessed=6 * steps * B * B, transcendentals=0
        ),
        compiler_params=pltpu.CompilerParams(vmem_limit_bytes=58 << 20),
        name="prepare",
    )(block_ranks, diag_inv, left_t, right_t, rates[:, None, :], *kept)


def prefix_kernel(step, side, out):
    moved = None
    for k in range(step.shape[0]):
        cols = slice(k * B, (k + 1) * B)
        if moved is None:
            out[:, cols] = side[:, cols]
            moved = step[k].T
        else:
            out[:, cols] = dot3(moved, side[:, cols], 1, 0)
            if k + 1 < step.shape[0]:
                moved = dot3(moved, step[k], 1, 1)


def prefix_side(step, side):
    return pl.pallas_call(
        prefix_kernel,
        out_shape=jax.ShapeDtypeStruct(side.shape, f32),
        cost_estimate=pl.CostEstimate(
            flops=6 * R * side.size, bytes_accessed=8 * side.size, transcendentals=0
        ),
        compiler_params=pltpu.CompilerParams(vmem_limit_bytes=40 << 20),
        name="prefix",
    )(step, side)


def offset_kernel(grad, suffix_proj, transfer, out):
    found = dot3(grad[...], suffix_proj[...], 1, 1)
    high = found.astype(bf16).astype(f32)
    t = transfer[...]
    rows = jnp.concatenate(
        [
            jnp.concatenate([t[: R // 2], t[R // 2 :]], axis=1),
            jnp.concatenate([high, found - high], axis=1),
            jnp.zeros((8, 2 * R), f32),
        ]
    ).astype(bf16)
    for e in range(out.shape[0]):
        out[e] = rows


def offset_messages(grad, suffix_proj, transfer, count):
    return pl.pallas_call(
        offset_kernel,
        out_shape=jax.ShapeDtypeStruct((count, R // 2 + 16, 2 * R), bf16),
        compiler_params=pltpu.CompilerParams(vmem_limit_bytes=40 << 20),
        name="offset",
    )(grad, suffix_proj, transfer)


def local_kernel(grad, inverse, proj, step, side, solved, state):
    @pl.when(pl.program_id(0) == 0)
    def _():
        state[...] = jnp.zeros_like(state)

    g = grad[...]
    gh = g.astype(bf16).astype(f32)
    pair = jnp.concatenate([gh, g - gh]).astype(bf16)
    n = g.shape[0]

    def times(matrix):
        high, low = split(matrix)
        main = dot(pair, high, 1, 1)
        return (main[:n] + main[n:]) + dot(pair, low, 1, 1)[:n]

    entered = state[...]
    solved[...] = times(inverse[0]) - dot3(entered, side[...], 1, 0)
    state[...] = dot3(entered, step[0], 1, 1) + times(proj[...])


def local_solve(grad, diag_inv, proj, step, side):
    count = diag_inv.shape[0]
    labels = grad.shape[0]
    return pl.pallas_call(
        local_kernel,
        grid=(count,),
        in_specs=[
            pl.BlockSpec((labels, B), lambda i: (0, i)),
            pl.BlockSpec((1, B, B), lambda i: (i, 0, 0)),
            pl.BlockSpec((R, B), lambda i: (0, i)),
            pl.BlockSpec((1, R, R), lambda i: (i, 0, 0)),
            pl.BlockSpec((R, B), lambda i: (0, i)),
        ],
        out_specs=pl.BlockSpec((labels, B), lambda i: (0, i)),
        out_shape=jax.ShapeDtypeStruct((labels, count * B), f32),
        scratch_shapes=[pltpu.VMEM((labels, R), f32)],
        cost_estimate=pl.CostEstimate(
            flops=6 * count * labels * B * B, bytes_accessed=4 * count * B * B, transcendentals=0
        ),
        compiler_params=pltpu.CompilerParams(vmem_limit_bytes=56 << 20),
        name="local_solve",
    )(grad, diag_inv, proj, step, side)


def finish_kernel(place, messages, solved, side, out):
    mine = place[0]
    count = messages.shape[0]
    half = R // 2

    def read(e):
        got = messages[e].astype(f32)
        transfer = jnp.concatenate([got[:half, :R], got[:half, R:]]).astype(bf16)
        rows = got[half : half + 8]
        return transfer, rows[:, :R] + rows[:, R:]

    def apply(rows, transfer):
        high, low = split(rows)
        return dot(high, transfer, 1, 1) + dot(low, transfer, 1, 1)

    eye = lax.broadcasted_iota(jnp.int32, (R, R), 0) == lax.broadcasted_iota(jnp.int32, (R, R), 1)
    early = jnp.zeros((8, R), f32)
    late = jnp.concatenate([early, eye.astype(f32)])
    blank = jnp.zeros((R, R), f32)
    for e in range(count // 2):
        transfer, rows = read(e)
        early = jnp.where(e < mine, apply(early, transfer) + rows, early)
        f = e + count // 2
        transfer, rows = read(f)
        moved = apply(late, transfer) + jnp.concatenate([rows, blank])
        late = jnp.where(f < mine, moved, late)
    entering = late[:8] + dot3(early, late[8:], 1, 0)
    z = solved[...] - dot3(entering, side[...], 1, 0)
    top = jnp.max(jnp.abs(z), axis=1, keepdims=True)
    power = jnp.ceil(jnp.log2(jnp.maximum(top, 1e-30)))
    width = z.shape[1]
    out[:, :width] = z * jnp.exp2(-power)
    out[:, width:] = jnp.broadcast_to(power, (8, 2 * R))


def finish(place, messages, solved, side):
    labels, m = solved.shape
    return pl.pallas_call(
        finish_kernel,
        grid_spec=pltpu.PrefetchScalarGridSpec(
            num_scalar_prefetch=1,
            grid=(),
            in_specs=[vmem, vmem, vmem],
            out_specs=vmem,
        ),
        out_shape=jax.ShapeDtypeStruct((labels, m + 2 * R), f32),
        compiler_params=pltpu.CompilerParams(vmem_limit_bytes=40 << 20),
        name="finish",
    )(place.reshape(1), messages, solved, side)


def unscaled_kernel(powers, scaled, out):
    out[...] = (scaled[...] * jnp.exp2(powers[:, :1])).T


def unscaled(whole, cols=1024):
    labels = whole.shape[0]
    m = whole.shape[1] - 2 * R
    return pl.pallas_call(
        unscaled_kernel,
        grid=(m // cols,),
        in_specs=[
            pl.BlockSpec((labels, 2 * R), lambda i: (0, m // (2 * R))),
            pl.BlockSpec((labels, cols), lambda i: (0, i)),
        ],
        out_specs=pl.BlockSpec((cols, labels), lambda i: (i, 0)),
        out_shape=jax.ShapeDtypeStruct((m, labels), f32),
        compiler_params=pltpu.CompilerParams(vmem_limit_bytes=40 << 20),
        name="unscaled",
    )(whole, whole)


def sent_to_all(array, axis):
    copies = jnp.broadcast_to(array, (lax.axis_size(axis), *array.shape))
    return lax.all_to_all(copies, axis, split_axis=0, concat_axis=0, tiled=True)


def to_partner(array):
    return lax.ppermute(array, "c", [(0, 1), (1, 0)])


def body(points, centers, coeffs, targets, diag_inv, low_left, low_right, decay_rates, block_ranks):
    n, labels = targets.shape
    m = centers.shape[0]
    chips, samp = lax.axis_size("z"), lax.axis_size("samp")
    chip, core = lax.axis_index("z"), lax.axis_index("c")
    place = chip * 2 + core
    share = n // (2 * chips)

    first = core * (n // 2) + chip * share
    own_targets = lax.dynamic_slice_in_dim(targets, first, share, 0)
    points, own_targets = lax.optimization_barrier((points, own_targets))
    in_hbm = lambda array: pltpu.with_memory_space_constraint(array, pltpu.HBM)
    diag_inv, points_t, centers_t = in_hbm(diag_inv), in_hbm(points.T), in_hbm(centers.T)
    stored_b, pred_b, extended, coeffs_v = predict(
        1 - core, points_t, centers_t, in_hbm(coeffs), True
    )
    from_partner = to_partner(pred_b)
    stored_a, pred_a = predict(core, points_t, extended, coeffs_v, False)
    pair_sum = (pred_a + from_partner).astype(wire).reshape(chips, share, labels)
    arrived = lax.all_to_all(pair_sum, "z", 0, 0, tiled=True)
    pred_own = arrived.astype(f32).sum(axis=0)
    resid = (jax.nn.sigmoid(pred_own) - own_targets.astype(f32)).astype(bf16)
    resid_a = sent_to_all(resid, "z").reshape(n // 2, labels)
    resid_b = to_partner(resid_a)

    partial = gradient_t(resid_a, resid_b, stored_a, stored_b)
    own = labels // samp
    sent = partial.astype(wire).reshape(samp, own, m)
    sent, block_ranks = lax.optimization_barrier((sent, block_ranks))
    arrived = lax.all_to_all(sent, "samp", 0, 0, tiled=True)
    prepared = prepare(
        block_ranks,
        diag_inv,
        jnp.swapaxes(low_left, 1, 2),
        jnp.swapaxes(low_right, 1, 2),
        decay_rates,
    )
    side_prefix = prefix_side(prepared[1], prepared[2])
    arrived, prepared, side_prefix = lax.optimization_barrier((arrived, prepared, side_prefix))
    proj, step, side, suffix_proj, transfer = prepared
    own_coeffs = lax.dynamic_slice_in_dim(coeffs, lax.axis_index("samp") * own, own, 1).T
    scaling = 1.0 / math.sqrt(n * samp)
    grad = arrived.astype(f32).sum(axis=0) * scaling + ridge_weight * own_coeffs.astype(f32)

    messages = offset_messages(grad, suffix_proj, transfer, 2 * chips)
    messages = lax.all_to_all(messages, ("z", "c"), 0, 0, tiled=True)
    solved = local_solve(grad, diag_inv, proj, step, side)
    direction = finish(place, messages, solved, side_prefix)
    whole = sent_to_all(direction.astype(wire), "samp").reshape(labels, m + 2 * R)
    return unscaled(whole.astype(f32))


def solution(mesh):
    finer = Mesh(mesh.devices.reshape(mesh.shape["samp"], -1, 2), ("samp", "z", "c"))
    ind = ("z", "c")
    placed = (
        P("samp", None),
        P(ind, None),
        P(ind, None),
        P("samp", None),
        P(ind, None, None),
        P(ind, None, None),
        P(ind, None, None),
        P(ind, None),
        P(ind),
    )
    return jax.shard_map(
        body, mesh=finer, in_specs=placed, out_specs=P(ind, None), check_vma=False
    )
```

```python
import functools
import math

import jax
import jax.numpy as jnp
from jax import lax
from jax.experimental import pallas as pl
from jax.experimental.pallas import tpu as pltpu
from jax.sharding import Mesh
from jax.sharding import PartitionSpec as P

D = 64
B = 512
R = 64
NB = 128
LOG2E = math.log2(math.e)

f32 = jnp.float32
bf16 = jnp.bfloat16
wire = jnp.float16
ridge_weight = 0.1
highest = lax.Precision.HIGHEST


def dot(a, b, ca, cb):
    return lax.dot_general(a, b, (((ca,), (cb,)), ((), ())), preferred_element_type=f32)


def split(a):
    high = a.astype(bf16)
    return high, (a - high.astype(f32)).astype(bf16)


def dot3(a, b, ca, cb):
    ah, al = split(a)
    bh, bl = split(b)
    return dot(ah, bh, ca, cb) + (dot(ah, bl, ca, cb) + dot(al, bh, ca, cb))


def with_norms(columns, left):
    half = jnp.sum(columns * columns, axis=0, keepdims=True) * -0.5
    high = half.astype(bf16).astype(f32)
    rest = half - high
    middle = rest.astype(bf16).astype(f32)
    n = columns.shape[1]
    ones = [jnp.ones((1, n), f32)] * 3
    parts = [high, middle, rest - middle]
    extra = parts + ones if left else ones + parts
    return jnp.concatenate([columns, *extra, jnp.zeros((2, n), f32)])


def predict_kernel(width, half, points_t, centers, coeffs, stored, pred, *kept):
    i = pl.program_id(0)
    rows = pred.shape[0]
    if kept:
        centers_t, (centers, coeffs_v) = centers, kept

        @pl.when(i == 0)
        def _():
            centers[...] = with_norms(centers_t[...].astype(f32), False).astype(bf16)
            coeffs_v[...] = coeffs[...]

    x = with_norms(points_t[...].astype(f32), True).T.astype(bf16)
    here = pl.ds(pl.multiple_of(i * rows, rows), rows)
    total = None
    for at in range(0, centers.shape[1], width):
        scaled = dot(x, centers[:, at : at + width], 1, 0) * (2 * LOG2E / D)
        k = jnp.exp2(scaled).astype(bf16)
        stored[here, at : at + width] = k
        part = dot(k, coeffs[at : at + width, :], 1, 0)
        total = part if total is None else total + part
    pred[...] = total


vmem = pl.BlockSpec(memory_space=pltpu.VMEM)


def predict(half, points_t, centers, coeffs, first, rows=1024, width=256):
    n, m, labels = points_t.shape[1] // 2, centers.shape[1], coeffs.shape[1]
    steps = n // rows
    whole = lambda i, half: (0, 0)
    outs = [pltpu.VMEM((n, m), bf16), jax.ShapeDtypeStruct((n, labels), f32)]
    if first:
        outs += [pltpu.VMEM((D + 8, m), bf16), pltpu.VMEM((m, labels), bf16)]
    return pl.pallas_call(
        functools.partial(predict_kernel, width),
        grid_spec=pltpu.PrefetchScalarGridSpec(
            num_scalar_prefetch=1,
            grid=(steps,),
            in_specs=[pl.BlockSpec((D, rows), lambda i, half: (0, half[0] * steps + i))]
            + (
                [pl.BlockSpec((D, m), whole), pl.BlockSpec((m, labels), whole)]
                if first
                else [vmem, vmem]
            ),
            out_specs=[vmem, pl.BlockSpec((rows, labels), lambda i, half: (i, 0))]
            + ([vmem, vmem] if first else []),
        ),
        out_shape=outs,
        compiler_params=pltpu.CompilerParams(vmem_limit_bytes=20 << 20),
        cost_estimate=pl.CostEstimate(
            flops=2 * n * m * (D + labels), bytes_accessed=2 * n * m, transcendentals=n * m
        ),
        name="predict",
    )(half.reshape(1), points_t, centers, coeffs)


def residual_kernel(share_at, pred, targets, out):
    resid = (jax.nn.sigmoid(pred[...]) - targets[...].astype(f32)).astype(bf16)
    for e in range(out.shape[0]):
        out[e] = resid


def residual_copies(share_at, pred, targets, copies):
    n, labels = pred.shape
    return pl.pallas_call(
        residual_kernel,
        grid_spec=pltpu.PrefetchScalarGridSpec(
            num_scalar_prefetch=1,
            grid=(1,),
            in_specs=[
                pl.BlockSpec((n, labels), lambda i, share_at: (0, 0)),
                pl.BlockSpec((n, labels), lambda i, share_at: (share_at[0], 0)),
            ],
            out_specs=pl.BlockSpec((copies, n, labels), lambda i, share_at: (0, 0, 0)),
        ),
        out_shape=jax.ShapeDtypeStruct((copies, n, labels), bf16),
        compiler_params=pltpu.CompilerParams(vmem_limit_bytes=8 << 20),
        name="residual",
    )(share_at.reshape(1), pred, targets)


def gradient_kernel(resid, rows, *refs):
    *earlier, out, turned = refs
    i = pl.program_id(0)

    @pl.when(i == 0)
    def _():
        turned[...] = resid[...].astype(f32).T.astype(bf16)

    cols = out.shape[1] // pl.num_programs(0)
    here = pl.ds(pl.multiple_of(i * cols, cols), cols)
    part = dot(turned[...], rows[:, here], 1, 0)
    out[:, here] = earlier[0][:, here] + part if earlier else part


def gradient_t(resid, stored, *earlier, cols=2048):
    n, labels = resid.shape
    m = stored.shape[1]
    return pl.pallas_call(
        gradient_kernel,
        grid=(m // cols,),
        in_specs=[vmem] * (2 + len(earlier)),
        out_specs=vmem,
        out_shape=pltpu.VMEM((labels, m), f32),
        scratch_shapes=[pltpu.VMEM((labels, n), bf16)],
        compiler_params=pltpu.CompilerParams(vmem_limit_bytes=16 << 20),
        cost_estimate=pl.CostEstimate(
            flops=2 * n * m * labels, bytes_accessed=2 * n * m, transcendentals=0
        ),
        name="gradient",
    )(resid, stored, *earlier)


def prepare_kernel(
    last, ranks, inverse, left_t, right_t, rates, proj, step, side, suffix_proj, transfer, acc
):
    i = pl.program_id(0)
    eye = lax.broadcasted_iota(jnp.int32, (R, R), 0) == lax.broadcasted_iota(jnp.int32, (R, R), 1)

    @pl.when(i == 0)
    def _():
        acc[...] = eye.astype(f32)

    kept = lax.broadcasted_iota(jnp.int32, (R, B), 0) < ranks[last - i]
    left = jnp.where(kept, left_t[0].astype(f32), 0.0).astype(bf16)
    right = jnp.where(kept, right_t[0].astype(f32), 0.0).astype(bf16)
    high, low = split(inverse[0])
    p = dot(right, high, 1, 0) + dot(right, low, 1, 0)
    proj[...] = p
    side[...] = dot(left, high, 1, 1) + dot(left, low, 1, 1)
    ph, plow = split(p)
    decay = jnp.exp(rates[0] * (-1.0 / NB))
    a = jnp.where(eye, decay, 0.0) - (dot(ph, left, 1, 1) + dot(plow, left, 1, 1))
    step[0] = a
    suffix = acc[...]
    suffix_proj[...] = dot3(suffix, p, 1, 0)
    suffix = jnp.dot(suffix, a, precision=highest, preferred_element_type=f32)
    acc[...] = suffix
    transfer[...] = suffix


def prepare(block_ranks, diag_inv, left_t, right_t, rates):
    count = diag_inv.shape[0]
    last = count - 1
    back = lambda i, ranks: (last - i, 0, 0)
    wide = lambda i, ranks: (0, last - i)
    wide_shape = jax.ShapeDtypeStruct((R, count * B), f32)
    return pl.pallas_call(
        functools.partial(prepare_kernel, last),
        grid_spec=pltpu.PrefetchScalarGridSpec(
            num_scalar_prefetch=1,
            grid=(count,),
            in_specs=[
                pl.BlockSpec((1, B, B), back),
                pl.BlockSpec((1, R, B), back),
                pl.BlockSpec((1, R, B), back),
                pl.BlockSpec((1, 1, R), back),
            ],
            out_specs=[
                pl.BlockSpec((R, B), wide),
                pl.BlockSpec((1, R, R), back),
                pl.BlockSpec((R, B), wide),
                pl.BlockSpec((R, B), wide),
                pl.BlockSpec((R, R), lambda i, ranks: (0, 0)),
            ],
            scratch_shapes=[pltpu.VMEM((R, R), f32)],
        ),
        out_shape=[
            wide_shape,
            jax.ShapeDtypeStruct((count, R, R), f32),
            wide_shape,
            wide_shape,
            jax.ShapeDtypeStruct((R, R), f32),
        ],
        cost_estimate=pl.CostEstimate(
            flops=8 * count * R * B * B, bytes_accessed=6 * count * B * B, transcendentals=0
        ),
        compiler_params=pltpu.CompilerParams(vmem_limit_bytes=24 << 20),
        name="prepare",
    )(block_ranks, diag_inv, left_t, right_t, rates[:, None, :])


def prefix_kernel(step, side, out):
    moved = None
    for k in range(step.shape[0]):
        cols = slice(k * B, (k + 1) * B)
        if moved is None:
            out[:, cols] = side[:, cols]
            moved = step[k].T
        else:
            out[:, cols] = dot3(moved, side[:, cols], 1, 0)
            if k + 1 < step.shape[0]:
                moved = dot3(moved, step[k], 1, 1)


def prefix_side(step, side):
    return pl.pallas_call(
        prefix_kernel,
        out_shape=jax.ShapeDtypeStruct(side.shape, f32),
        cost_estimate=pl.CostEstimate(
            flops=6 * R * side.size, bytes_accessed=8 * side.size, transcendentals=0
        ),
        compiler_params=pltpu.CompilerParams(vmem_limit_bytes=40 << 20),
        name="prefix",
    )(step, side)


def offset_kernel(grad, suffix_proj, transfer, out):
    found = dot3(grad[...], suffix_proj[...], 1, 1)
    high = found.astype(bf16).astype(f32)
    t = transfer[...]
    rows = jnp.concatenate(
        [
            jnp.concatenate([t[: R // 2], t[R // 2 :]], axis=1),
            jnp.concatenate([high, found - high], axis=1),
            jnp.zeros((8, 2 * R), f32),
        ]
    ).astype(bf16)
    for e in range(out.shape[0]):
        out[e] = rows


def offset_messages(grad, suffix_proj, transfer, count):
    return pl.pallas_call(
        offset_kernel,
        out_shape=jax.ShapeDtypeStruct((count, R // 2 + 16, 2 * R), bf16),
        compiler_params=pltpu.CompilerParams(vmem_limit_bytes=58 << 20),
        name="offset",
    )(grad, suffix_proj, transfer)


def local_kernel(grad, inverse, proj, step, side, solved, state):
    @pl.when(pl.program_id(0) == 0)
    def _():
        state[...] = jnp.zeros_like(state)

    g = grad[...]
    gh = g.astype(bf16).astype(f32)
    pair = jnp.concatenate([gh, g - gh]).astype(bf16)
    n = g.shape[0]

    def times(matrix):
        high, low = split(matrix)
        main = dot(pair, high, 1, 1)
        return (main[:n] + main[n:]) + dot(pair, low, 1, 1)[:n]

    entered = state[...]
    solved[...] = times(inverse[0]) - dot3(entered, side[...], 1, 0)
    state[...] = dot3(entered, step[0], 1, 1) + times(proj[...])


def local_solve(grad, diag_inv, proj, step, side):
    count = diag_inv.shape[0]
    labels = grad.shape[0]
    return pl.pallas_call(
        local_kernel,
        grid=(count,),
        in_specs=[
            pl.BlockSpec((labels, B), lambda i: (0, i)),
            pl.BlockSpec((1, B, B), lambda i: (i, 0, 0)),
            pl.BlockSpec((R, B), lambda i: (0, i)),
            pl.BlockSpec((1, R, R), lambda i: (i, 0, 0)),
            pl.BlockSpec((R, B), lambda i: (0, i)),
        ],
        out_specs=pl.BlockSpec((labels, B), lambda i: (0, i)),
        out_shape=jax.ShapeDtypeStruct((labels, count * B), f32),
        scratch_shapes=[pltpu.VMEM((labels, R), f32)],
        cost_estimate=pl.CostEstimate(
            flops=6 * count * labels * B * B, bytes_accessed=4 * count * B * B, transcendentals=0
        ),
        compiler_params=pltpu.CompilerParams(vmem_limit_bytes=24 << 20),
        name="local_solve",
    )(grad, diag_inv, proj, step, side)


def finish_kernel(place, messages, solved, side, out):
    mine = place[0]
    count = messages.shape[0]
    half = R // 2

    def read(e):
        got = messages[e].astype(f32)
        transfer = jnp.concatenate([got[:half, :R], got[:half, R:]]).astype(bf16)
        rows = got[half : half + 8]
        return transfer, rows[:, :R] + rows[:, R:]

    def apply(rows, transfer):
        high, low = split(rows)
        return dot(high, transfer, 1, 1) + dot(low, transfer, 1, 1)

    eye = lax.broadcasted_iota(jnp.int32, (R, R), 0) == lax.broadcasted_iota(jnp.int32, (R, R), 1)
    early = jnp.zeros((8, R), f32)
    late = jnp.concatenate([early, eye.astype(f32)])
    blank = jnp.zeros((R, R), f32)
    for e in range(count // 2):
        transfer, rows = read(e)
        early = jnp.where(e < mine, apply(early, transfer) + rows, early)
        f = e + count // 2
        transfer, rows = read(f)
        moved = apply(late, transfer) + jnp.concatenate([rows, blank])
        late = jnp.where(f < mine, moved, late)
    entering = late[:8] + dot3(early, late[8:], 1, 0)
    z = solved[...] - dot3(entering, side[...], 1, 0)
    top = jnp.max(jnp.abs(z), axis=1, keepdims=True)
    power = jnp.ceil(jnp.log2(jnp.maximum(top, 1e-30)))
    width = z.shape[1]
    out[:, :width] = z * jnp.exp2(-power)
    out[:, width:] = jnp.broadcast_to(power, (8, 2 * R))


def finish(place, messages, solved, side):
    labels, m = solved.shape
    return pl.pallas_call(
        finish_kernel,
        grid_spec=pltpu.PrefetchScalarGridSpec(
            num_scalar_prefetch=1,
            grid=(),
            in_specs=[vmem, vmem, vmem],
            out_specs=vmem,
        ),
        out_shape=jax.ShapeDtypeStruct((labels, m + 2 * R), f32),
        compiler_params=pltpu.CompilerParams(vmem_limit_bytes=40 << 20),
        name="finish",
    )(place.reshape(1), messages, solved, side)


def unscaled_kernel(powers, scaled, out):
    out[...] = (scaled[...] * jnp.exp2(powers[:, :1])).T


def unscaled(whole, cols=1024):
    labels = whole.shape[0]
    m = whole.shape[1] - 2 * R
    return pl.pallas_call(
        unscaled_kernel,
        grid=(m // cols,),
        in_specs=[
            pl.BlockSpec((labels, 2 * R), lambda i: (0, m // (2 * R))),
            pl.BlockSpec((labels, cols), lambda i: (0, i)),
        ],
        out_specs=pl.BlockSpec((cols, labels), lambda i: (i, 0)),
        out_shape=jax.ShapeDtypeStruct((m, labels), f32),
        compiler_params=pltpu.CompilerParams(vmem_limit_bytes=40 << 20),
        name="unscaled",
    )(whole, whole)


def sent_to_all(array, axis):
    copies = jnp.broadcast_to(array, (lax.axis_size(axis), *array.shape))
    return lax.all_to_all(copies, axis, split_axis=0, concat_axis=0, tiled=True)


def to_partner(array):
    return lax.ppermute(array, "c", [(0, 1), (1, 0)])


def body(points, centers, coeffs, targets, diag_inv, low_left, low_right, decay_rates, block_ranks):
    n, labels = targets.shape
    m = centers.shape[0]
    chips, samp = lax.axis_size("z"), lax.axis_size("samp")
    chip, core = lax.axis_index("z"), lax.axis_index("c")
    place = chip * 2 + core
    share = n // (2 * chips)

    in_hbm = lambda array: pltpu.with_memory_space_constraint(array, pltpu.HBM)
    points, share_at, place = lax.optimization_barrier((points, core * chips + chip, place))
    diag_inv, points_t, centers_t = in_hbm(diag_inv), in_hbm(points.T), in_hbm(centers.T)
    stored_b, pred_b, extended, coeffs_v = predict(
        1 - core, points_t, centers_t, in_hbm(coeffs), True
    )
    from_partner = to_partner(pred_b)
    stored_a, pred_a = predict(core, points_t, extended, coeffs_v, False)
    pair_sum = (pred_a + from_partner).astype(wire).reshape(chips, share, labels)
    arrived = lax.all_to_all(pair_sum, "z", 0, 0, tiled=True)
    pred_own = arrived.astype(f32).sum(axis=0)
    resid = residual_copies(share_at, pred_own, in_hbm(targets), chips)
    resid_a = lax.all_to_all(resid, "z", 0, 0, tiled=True).reshape(n // 2, labels)
    resid_b = to_partner(resid_a)

    partial = gradient_t(resid_a, stored_a)
    partial = gradient_t(resid_b, stored_b, partial)
    own = labels // samp
    sent = partial.astype(wire).reshape(samp, own, m)
    sent, block_ranks = lax.optimization_barrier((sent, block_ranks))
    arrived = lax.all_to_all(sent, "samp", 0, 0, tiled=True)
    prepared = prepare(
        block_ranks,
        diag_inv,
        jnp.swapaxes(low_left, 1, 2),
        jnp.swapaxes(low_right, 1, 2),
        decay_rates,
    )
    side_prefix = prefix_side(prepared[1], prepared[2])
    arrived, prepared, side_prefix = lax.optimization_barrier((arrived, prepared, side_prefix))
    proj, step, side, suffix_proj, transfer = prepared
    own_coeffs = lax.dynamic_slice_in_dim(coeffs, lax.axis_index("samp") * own, own, 1).T
    scaling = 1.0 / math.sqrt(n * samp)
    grad = arrived.astype(f32).sum(axis=0) * scaling + ridge_weight * own_coeffs.astype(f32)

    messages = offset_messages(grad, suffix_proj, transfer, 2 * chips)
    messages = lax.all_to_all(messages, ("z", "c"), 0, 0, tiled=True)
    solved = local_solve(grad, diag_inv, proj, step, side)
    direction = finish(place, messages, solved, side_prefix)
    whole = sent_to_all(direction.astype(wire), "samp").reshape(labels, m + 2 * R)
    return unscaled(whole.astype(f32))


def solution(mesh):
    finer = Mesh(mesh.devices.reshape(mesh.shape["samp"], -1, 2), ("samp", "z", "c"))
    ind = ("z", "c")
    placed = (
        P("samp", None),
        P(ind, None),
        P(ind, None),
        P("samp", None),
        P(ind, None, None),
        P(ind, None, None),
        P(ind, None, None),
        P(ind, None),
        P(ind),
    )
    return jax.shard_map(
        body, mesh=finer, in_specs=placed, out_specs=P(ind, None), check_vma=False
    )
```

```python
import functools
import math

import jax
import jax.numpy as jnp
from jax import lax
from jax.experimental import pallas as pl
from jax.experimental.pallas import tpu as pltpu
from jax.sharding import Mesh
from jax.sharding import PartitionSpec as P

D = 64
B = 512
R = 64
NB = 128
LOG2E = math.log2(math.e)

f32 = jnp.float32
bf16 = jnp.bfloat16
wire = jnp.float16
ridge_weight = 0.1
highest = lax.Precision.HIGHEST


def dot(a, b, ca, cb):
    return lax.dot_general(a, b, (((ca,), (cb,)), ((), ())), preferred_element_type=f32)


def split(a):
    high = a.astype(bf16)
    return high, (a - high.astype(f32)).astype(bf16)


def dot3(a, b, ca, cb):
    ah, al = split(a)
    bh, bl = split(b)
    return dot(ah, bh, ca, cb) + (dot(ah, bl, ca, cb) + dot(al, bh, ca, cb))


def with_norms(columns, left):
    half = jnp.sum(columns * columns, axis=0, keepdims=True) * -0.5
    high = half.astype(bf16).astype(f32)
    rest = half - high
    middle = rest.astype(bf16).astype(f32)
    n = columns.shape[1]
    ones = [jnp.ones((1, n), f32)] * 3
    parts = [high, middle, rest - middle]
    extra = parts + ones if left else ones + parts
    return jnp.concatenate([columns, *extra, jnp.zeros((2, n), f32)])


def predict_kernel(width, half, points_t, centers, coeffs, stored, pred, *kept):
    arriving = None
    if kept:
        centers_t, (centers, coeffs_v, arrived) = centers, kept
        arriving = pltpu.make_async_copy(coeffs, coeffs_v, arrived)
        arriving.start()
        centers[...] = with_norms(centers_t[...].astype(f32), False).astype(bf16)
        coeffs = coeffs_v

    x = with_norms(points_t[...].astype(f32), True).T.astype(bf16)
    total = None
    for at in range(0, centers.shape[1], width):
        scaled = dot(x, centers[:, at : at + width], 1, 0) * (2 * LOG2E / D)
        k = jnp.exp2(scaled).astype(bf16)
        stored[:, at : at + width] = k
        if arriving is not None and at == 0:
            arriving.wait()
        part = dot(k, coeffs[at : at + width, :], 1, 0)
        total = part if total is None else total + part
    pred[...] = total


vmem = pl.BlockSpec(memory_space=pltpu.VMEM)


def predict(half, points_t, centers, coeffs, first, width=256):
    n, m, labels = points_t.shape[1] // 2, centers.shape[1], coeffs.shape[1]
    whole = lambda i, half: (0, 0)
    outs = [pltpu.VMEM((n, m), bf16), jax.ShapeDtypeStruct((n, labels), f32)]
    if first:
        outs += [pltpu.VMEM((D + 8, m), bf16), pltpu.VMEM((m, labels), bf16)]
    return pl.pallas_call(
        functools.partial(predict_kernel, width),
        grid_spec=pltpu.PrefetchScalarGridSpec(
            num_scalar_prefetch=1,
            grid=(1,),
            in_specs=[pl.BlockSpec((D, n), lambda i, half: (0, half[0]))]
            + (
                [pl.BlockSpec((D, m), whole), pl.BlockSpec(memory_space=pl.ANY)]
                if first
                else [vmem, vmem]
            ),
            out_specs=[vmem, pl.BlockSpec((n, labels), lambda i, half: (0, 0))]
            + ([vmem, vmem] if first else []),
            scratch_shapes=[pltpu.SemaphoreType.DMA] if first else [],
        ),
        out_shape=outs,
        compiler_params=pltpu.CompilerParams(vmem_limit_bytes=20 << 20),
        cost_estimate=pl.CostEstimate(
            flops=2 * n * m * (D + labels), bytes_accessed=2 * n * m, transcendentals=n * m
        ),
        name="predict",
    )(half.reshape(1), points_t, centers, coeffs)


def residual_kernel(share_at, pred, targets, out):
    resid = (jax.nn.sigmoid(pred[...]) - targets[...].astype(f32)).astype(bf16)
    for e in range(out.shape[0]):
        out[e] = resid


def residual_copies(share_at, pred, targets, copies):
    n, labels = pred.shape
    return pl.pallas_call(
        residual_kernel,
        grid_spec=pltpu.PrefetchScalarGridSpec(
            num_scalar_prefetch=1,
            grid=(1,),
            in_specs=[
                pl.BlockSpec((n, labels), lambda i, share_at: (0, 0)),
                pl.BlockSpec((n, labels), lambda i, share_at: (share_at[0], 0)),
            ],
            out_specs=pl.BlockSpec((copies, n, labels), lambda i, share_at: (0, 0, 0)),
        ),
        out_shape=jax.ShapeDtypeStruct((copies, n, labels), bf16),
        compiler_params=pltpu.CompilerParams(vmem_limit_bytes=8 << 20),
        name="residual",
    )(share_at.reshape(1), pred, targets)


def gradient_kernel(resid, rows, *refs):
    *earlier, out, turned = refs
    i = pl.program_id(0)

    @pl.when(i == 0)
    def _():
        turned[...] = resid[...].astype(f32).T.astype(bf16)

    cols = out.shape[1] // pl.num_programs(0)
    here = pl.ds(pl.multiple_of(i * cols, cols), cols)
    part = dot(turned[...], rows[:, here], 1, 0)
    out[:, here] = earlier[0][:, here] + part if earlier else part


def gradient_t(resid, stored, *earlier, cols=2048):
    n, labels = resid.shape
    m = stored.shape[1]
    return pl.pallas_call(
        gradient_kernel,
        grid=(m // cols,),
        in_specs=[vmem] * (2 + len(earlier)),
        out_specs=vmem,
        out_shape=pltpu.VMEM((labels, m), f32),
        scratch_shapes=[pltpu.VMEM((labels, n), bf16)],
        compiler_params=pltpu.CompilerParams(vmem_limit_bytes=16 << 20),
        cost_estimate=pl.CostEstimate(
            flops=2 * n * m * labels, bytes_accessed=2 * n * m, transcendentals=0
        ),
        name="gradient",
    )(resid, stored, *earlier)


def prepare_kernel(
    last, ranks, inverse, left_t, right_t, rates, proj, step, side, suffix_proj, transfer, acc
):
    i = pl.program_id(0)
    eye = lax.broadcasted_iota(jnp.int32, (R, R), 0) == lax.broadcasted_iota(jnp.int32, (R, R), 1)

    @pl.when(i == 0)
    def _():
        acc[...] = eye.astype(f32)

    kept = lax.broadcasted_iota(jnp.int32, (R, B), 0) < ranks[last - i]
    left = jnp.where(kept, left_t[0].astype(f32), 0.0).astype(bf16)
    right = jnp.where(kept, right_t[0].astype(f32), 0.0).astype(bf16)
    high, low = split(inverse[0])
    p = dot(right, high, 1, 0) + dot(right, low, 1, 0)
    proj[...] = p
    side[...] = dot(left, high, 1, 1) + dot(left, low, 1, 1)
    ph, plow = split(p)
    decay = jnp.exp(rates[0] * (-1.0 / NB))
    a = jnp.where(eye, decay, 0.0) - (dot(ph, left, 1, 1) + dot(plow, left, 1, 1))
    step[0] = a
    suffix = acc[...]
    suffix_proj[...] = dot3(suffix, p, 1, 0)
    suffix = jnp.dot(suffix, a, precision=highest, preferred_element_type=f32)
    acc[...] = suffix
    transfer[...] = suffix


def prepare(block_ranks, diag_inv, left_t, right_t, rates):
    count = diag_inv.shape[0]
    last = count - 1
    back = lambda i, ranks: (last - i, 0, 0)
    wide = lambda i, ranks: (0, last - i)
    wide_shape = jax.ShapeDtypeStruct((R, count * B), f32)
    return pl.pallas_call(
        functools.partial(prepare_kernel, last),
        grid_spec=pltpu.PrefetchScalarGridSpec(
            num_scalar_prefetch=1,
            grid=(count,),
            in_specs=[
                pl.BlockSpec((1, B, B), back),
                pl.BlockSpec((1, R, B), back),
                pl.BlockSpec((1, R, B), back),
                pl.BlockSpec((1, 1, R), back),
            ],
            out_specs=[
                pl.BlockSpec((R, B), wide),
                pl.BlockSpec((1, R, R), back),
                pl.BlockSpec((R, B), wide),
                pl.BlockSpec((R, B), wide),
                pl.BlockSpec((R, R), lambda i, ranks: (0, 0)),
            ],
            scratch_shapes=[pltpu.VMEM((R, R), f32)],
        ),
        out_shape=[
            wide_shape,
            jax.ShapeDtypeStruct((count, R, R), f32),
            wide_shape,
            wide_shape,
            jax.ShapeDtypeStruct((R, R), f32),
        ],
        cost_estimate=pl.CostEstimate(
            flops=8 * count * R * B * B, bytes_accessed=6 * count * B * B, transcendentals=0
        ),
        compiler_params=pltpu.CompilerParams(vmem_limit_bytes=24 << 20),
        name="prepare",
    )(block_ranks, diag_inv, left_t, right_t, rates[:, None, :])


def prefix_kernel(step, side, out):
    moved = None
    for k in range(step.shape[0]):
        cols = slice(k * B, (k + 1) * B)
        if moved is None:
            out[:, cols] = side[:, cols]
            moved = step[k].T
        else:
            out[:, cols] = dot3(moved, side[:, cols], 1, 0)
            if k + 1 < step.shape[0]:
                moved = dot3(moved, step[k], 1, 1)


def prefix_side(step, side):
    return pl.pallas_call(
        prefix_kernel,
        out_shape=jax.ShapeDtypeStruct(side.shape, f32),
        cost_estimate=pl.CostEstimate(
            flops=6 * R * side.size, bytes_accessed=8 * side.size, transcendentals=0
        ),
        compiler_params=pltpu.CompilerParams(vmem_limit_bytes=40 << 20),
        name="prefix",
    )(step, side)


def offset_kernel(grad, suffix_proj, transfer, out):
    found = dot3(grad[...], suffix_proj[...], 1, 1)
    high = found.astype(bf16).astype(f32)
    t = transfer[...]
    rows = jnp.concatenate(
        [
            jnp.concatenate([t[: R // 2], t[R // 2 :]], axis=1),
            jnp.concatenate([high, found - high], axis=1),
            jnp.zeros((8, 2 * R), f32),
        ]
    ).astype(bf16)
    for e in range(out.shape[0]):
        out[e] = rows


def offset_messages(grad, suffix_proj, transfer, count):
    return pl.pallas_call(
        offset_kernel,
        out_shape=pltpu.HBM((count, R // 2 + 16, 2 * R), bf16),
        compiler_params=pltpu.CompilerParams(vmem_limit_bytes=40 << 20),
        name="offset",
    )(grad, suffix_proj, transfer)


def local_kernel(grad, inverse, proj, step, side, solved, state):
    @pl.when(pl.program_id(0) == 0)
    def _():
        state[...] = jnp.zeros_like(state)

    g = grad[...]
    gh = g.astype(bf16).astype(f32)
    pair = jnp.concatenate([gh, g - gh]).astype(bf16)
    n = g.shape[0]

    def times(matrix):
        high, low = split(matrix)
        main = dot(pair, high, 1, 1)
        return (main[:n] + main[n:]) + dot(pair, low, 1, 1)[:n]

    entered = state[...]
    solved[...] = times(inverse[0]) - dot3(entered, side[...], 1, 0)
    state[...] = dot3(entered, step[0], 1, 1) + times(proj[...])


def local_solve(grad, diag_inv, proj, step, side):
    count = diag_inv.shape[0]
    labels = grad.shape[0]
    return pl.pallas_call(
        local_kernel,
        grid=(count,),
        in_specs=[
            pl.BlockSpec((labels, B), lambda i: (0, i)),
            pl.BlockSpec((1, B, B), lambda i: (i, 0, 0)),
            pl.BlockSpec((R, B), lambda i: (0, i)),
            pl.BlockSpec((1, R, R), lambda i: (i, 0, 0)),
            pl.BlockSpec((R, B), lambda i: (0, i)),
        ],
        out_specs=pl.BlockSpec((labels, B), lambda i: (0, i)),
        out_shape=jax.ShapeDtypeStruct((labels, count * B), f32),
        scratch_shapes=[pltpu.VMEM((labels, R), f32)],
        cost_estimate=pl.CostEstimate(
            flops=6 * count * labels * B * B, bytes_accessed=4 * count * B * B, transcendentals=0
        ),
        compiler_params=pltpu.CompilerParams(vmem_limit_bytes=40 << 20),
        name="local_solve",
    )(grad, diag_inv, proj, step, side)


def finish_kernel(place, messages, solved, side, out):
    mine = place[0]
    count = messages.shape[0]
    half = R // 2

    def read(e):
        got = messages[e].astype(f32)
        transfer = jnp.concatenate([got[:half, :R], got[:half, R:]]).astype(bf16)
        rows = got[half : half + 8]
        return transfer, rows[:, :R] + rows[:, R:]

    def apply(rows, transfer):
        high, low = split(rows)
        return dot(high, transfer, 1, 1) + dot(low, transfer, 1, 1)

    eye = lax.broadcasted_iota(jnp.int32, (R, R), 0) == lax.broadcasted_iota(jnp.int32, (R, R), 1)
    early = jnp.zeros((8, R), f32)
    late = jnp.concatenate([early, eye.astype(f32)])
    blank = jnp.zeros((R, R), f32)
    for e in range(count // 2):
        transfer, rows = read(e)
        early = jnp.where(e < mine, apply(early, transfer) + rows, early)
        f = e + count // 2
        transfer, rows = read(f)
        moved = apply(late, transfer) + jnp.concatenate([rows, blank])
        late = jnp.where(f < mine, moved, late)
    entering = late[:8] + dot3(early, late[8:], 1, 0)
    z = solved[...] - dot3(entering, side[...], 1, 0)
    top = jnp.max(jnp.abs(z), axis=1, keepdims=True)
    power = jnp.ceil(jnp.log2(jnp.maximum(top, 1e-30)))
    width = z.shape[1]
    out[:, :width] = z * jnp.exp2(-power)
    out[:, width:] = jnp.broadcast_to(power, (8, 2 * R))


def finish(place, messages, solved, side):
    labels, m = solved.shape
    return pl.pallas_call(
        finish_kernel,
        grid_spec=pltpu.PrefetchScalarGridSpec(
            num_scalar_prefetch=1,
            grid=(),
            in_specs=[vmem, vmem, vmem],
            out_specs=vmem,
        ),
        out_shape=jax.ShapeDtypeStruct((labels, m + 2 * R), f32),
        compiler_params=pltpu.CompilerParams(vmem_limit_bytes=40 << 20),
        name="finish",
    )(place.reshape(1), messages, solved, side)


def unscaled_kernel(powers, scaled, out):
    out[...] = (scaled[...] * jnp.exp2(powers[:, :1])).T


def unscaled(whole, cols=1024):
    labels = whole.shape[0]
    m = whole.shape[1] - 2 * R
    return pl.pallas_call(
        unscaled_kernel,
        grid=(m // cols,),
        in_specs=[
            pl.BlockSpec((labels, 2 * R), lambda i: (0, m // (2 * R))),
            pl.BlockSpec((labels, cols), lambda i: (0, i)),
        ],
        out_specs=pl.BlockSpec((cols, labels), lambda i: (i, 0)),
        out_shape=jax.ShapeDtypeStruct((m, labels), f32),
        compiler_params=pltpu.CompilerParams(vmem_limit_bytes=40 << 20),
        name="unscaled",
    )(whole, whole)


def sent_to_all(array, axis):
    copies = jnp.broadcast_to(array, (lax.axis_size(axis), *array.shape))
    return lax.all_to_all(copies, axis, split_axis=0, concat_axis=0, tiled=True)


def to_partner(array):
    return lax.ppermute(array, "c", [(0, 1), (1, 0)])


def body(points, centers, coeffs, targets, diag_inv, low_left, low_right, decay_rates, block_ranks):
    n, labels = targets.shape
    m = centers.shape[0]
    chips, samp = lax.axis_size("z"), lax.axis_size("samp")
    chip, core = lax.axis_index("z"), lax.axis_index("c")
    place = chip * 2 + core
    share = n // (2 * chips)

    in_hbm = lambda array: pltpu.with_memory_space_constraint(array, pltpu.HBM)
    points, share_at, place = lax.optimization_barrier((points, core * chips + chip, place))
    diag_inv, points_t, centers_t = in_hbm(diag_inv), in_hbm(points.T), in_hbm(centers.T)
    stored_b, pred_b, extended, coeffs_v = predict(
        1 - core, points_t, centers_t, in_hbm(coeffs), True
    )
    from_partner = to_partner(pred_b)
    stored_a, pred_a = predict(core, points_t, extended, coeffs_v, False)
    pair_sum = (pred_a + from_partner).astype(wire).reshape(chips, share, labels)
    arrived = lax.all_to_all(pair_sum, "z", 0, 0, tiled=True)
    pred_own = arrived.astype(f32).sum(axis=0)
    resid = residual_copies(share_at, pred_own, in_hbm(targets), chips)
    resid_a = lax.all_to_all(resid, "z", 0, 0, tiled=True).reshape(n // 2, labels)
    resid_b = to_partner(resid_a)

    partial = gradient_t(resid_a, stored_a)
    partial = gradient_t(resid_b, stored_b, partial)
    own = labels // samp
    sent = partial.astype(wire).reshape(samp, own, m)
    sent, block_ranks = lax.optimization_barrier((sent, block_ranks))
    arrived = lax.all_to_all(sent, "samp", 0, 0, tiled=True)
    prepared = prepare(
        block_ranks,
        diag_inv,
        jnp.swapaxes(low_left, 1, 2),
        jnp.swapaxes(low_right, 1, 2),
        decay_rates,
    )
    side_prefix = prefix_side(prepared[1], prepared[2])
    arrived, prepared, side_prefix = lax.optimization_barrier((arrived, prepared, side_prefix))
    proj, step, side, suffix_proj, transfer = prepared
    own_coeffs = lax.dynamic_slice_in_dim(coeffs, lax.axis_index("samp") * own, own, 1).T
    scaling = 1.0 / math.sqrt(n * samp)
    grad = arrived.astype(f32).sum(axis=0) * scaling + ridge_weight * own_coeffs.astype(f32)

    messages = offset_messages(grad, suffix_proj, transfer, 2 * chips)
    messages = lax.all_to_all(messages, ("z", "c"), 0, 0, tiled=True)
    solved = local_solve(grad, diag_inv, proj, step, side)
    direction = finish(place, messages, solved, side_prefix)
    whole = sent_to_all(direction.astype(wire), "samp").reshape(labels, m + 2 * R)
    return unscaled(whole.astype(f32))


def solution(mesh):
    finer = Mesh(mesh.devices.reshape(mesh.shape["samp"], -1, 2), ("samp", "z", "c"))
    ind = ("z", "c")
    placed = (
        P("samp", None),
        P(ind, None),
        P(ind, None),
        P("samp", None),
        P(ind, None, None),
        P(ind, None, None),
        P(ind, None, None),
        P(ind, None),
        P(ind),
    )
    return jax.shard_map(
        body, mesh=finer, in_specs=placed, out_specs=P(ind, None), check_vma=False
    )
```

```python
import functools
import math

import jax
import jax.numpy as jnp
from jax import lax
from jax.experimental import pallas as pl
from jax.experimental.pallas import tpu as pltpu
from jax.sharding import Mesh
from jax.sharding import PartitionSpec as P

D = 64
B = 512
R = 64
NB = 128
LOG2E = math.log2(math.e)

f32 = jnp.float32
bf16 = jnp.bfloat16
wire = jnp.float16
ridge_weight = 0.1
highest = lax.Precision.HIGHEST


def dot(a, b, ca, cb):
    return lax.dot_general(a, b, (((ca,), (cb,)), ((), ())), preferred_element_type=f32)


def split(a):
    high = a.astype(bf16)
    return high, (a - high.astype(f32)).astype(bf16)


def dot3(a, b, ca, cb):
    ah, al = split(a)
    bh, bl = split(b)
    return dot(ah, bh, ca, cb) + (dot(ah, bl, ca, cb) + dot(al, bh, ca, cb))


def with_norms(columns, left):
    half = jnp.sum(columns * columns, axis=0, keepdims=True) * -0.5
    high = half.astype(bf16).astype(f32)
    rest = half - high
    middle = rest.astype(bf16).astype(f32)
    n = columns.shape[1]
    ones = [jnp.ones((1, n), f32)] * 3
    parts = [high, middle, rest - middle]
    extra = parts + ones if left else ones + parts
    return jnp.concatenate([columns, *extra, jnp.zeros((2, n), f32)])


def predict_kernel(width, half, points_t, centers, coeffs, stored, pred, *kept):
    if kept:
        centers_t, (centers, coeffs_v) = centers, kept
        centers[...] = with_norms(centers_t[...].astype(f32), False).astype(bf16)
        coeffs_v[...] = coeffs[...]

    x = with_norms(points_t[...].astype(f32), True).T.astype(bf16)
    total = None
    for at in range(0, centers.shape[1], width):
        scaled = dot(x, centers[:, at : at + width], 1, 0) * (2 * LOG2E / D)
        k = jnp.exp2(scaled).astype(bf16)
        stored[:, at : at + width] = k
        part = dot(k, coeffs[at : at + width, :], 1, 0)
        total = part if total is None else total + part
    pred[...] = total


vmem = pl.BlockSpec(memory_space=pltpu.VMEM)


def predict(half, points_t, centers, coeffs, first, width=256):
    n, m, labels = points_t.shape[1] // 2, centers.shape[1], coeffs.shape[1]
    whole = lambda i, half: (0, 0)
    outs = [pltpu.VMEM((n, m), bf16), jax.ShapeDtypeStruct((n, labels), f32)]
    if first:
        outs += [pltpu.VMEM((D + 8, m), bf16), pltpu.VMEM((m, labels), bf16)]
    return pl.pallas_call(
        functools.partial(predict_kernel, width),
        grid_spec=pltpu.PrefetchScalarGridSpec(
            num_scalar_prefetch=1,
            grid=(1,),
            in_specs=[pl.BlockSpec((D, n), lambda i, half: (0, half[0]))]
            + (
                [pl.BlockSpec((D, m), whole), pl.BlockSpec((m, labels), whole)]
                if first
                else [vmem, vmem]
            ),
            out_specs=[vmem, pl.BlockSpec((n, labels), lambda i, half: (0, 0))]
            + ([vmem, vmem] if first else []),
        ),
        out_shape=outs,
        compiler_params=pltpu.CompilerParams(vmem_limit_bytes=20 << 20),
        cost_estimate=pl.CostEstimate(
            flops=2 * n * m * (D + labels), bytes_accessed=2 * n * m, transcendentals=n * m
        ),
        name="predict",
    )(half.reshape(1), points_t, centers, coeffs)


def residual_kernel(share_at, pred, targets, out):
    resid = (jax.nn.sigmoid(pred[...]) - targets[...].astype(f32)).astype(bf16)
    for e in range(out.shape[0]):
        out[e] = resid


def residual_copies(share_at, pred, targets, copies):
    n, labels = pred.shape
    return pl.pallas_call(
        residual_kernel,
        grid_spec=pltpu.PrefetchScalarGridSpec(
            num_scalar_prefetch=1,
            grid=(1,),
            in_specs=[
                pl.BlockSpec((n, labels), lambda i, share_at: (0, 0)),
                pl.BlockSpec((n, labels), lambda i, share_at: (share_at[0], 0)),
            ],
            out_specs=pl.BlockSpec((copies, n, labels), lambda i, share_at: (0, 0, 0)),
        ),
        out_shape=jax.ShapeDtypeStruct((copies, n, labels), bf16),
        compiler_params=pltpu.CompilerParams(vmem_limit_bytes=8 << 20),
        name="residual",
    )(share_at.reshape(1), pred, targets)


def gradient_kernel(resid, rows, *refs):
    *earlier, out, turned = refs
    i = pl.program_id(0)

    @pl.when(i == 0)
    def _():
        turned[...] = resid[...].astype(f32).T.astype(bf16)

    cols = out.shape[1] // pl.num_programs(0)
    here = pl.ds(pl.multiple_of(i * cols, cols), cols)
    part = dot(turned[...], rows[:, here], 1, 0)
    out[:, here] = earlier[0][:, here] + part if earlier else part


def gradient_t(resid, stored, *earlier, cols=2048):
    n, labels = resid.shape
    m = stored.shape[1]
    return pl.pallas_call(
        gradient_kernel,
        grid=(m // cols,),
        in_specs=[vmem] * (2 + len(earlier)),
        out_specs=vmem,
        out_shape=pltpu.VMEM((labels, m), f32),
        scratch_shapes=[pltpu.VMEM((labels, n), bf16)],
        compiler_params=pltpu.CompilerParams(vmem_limit_bytes=16 << 20),
        cost_estimate=pl.CostEstimate(
            flops=2 * n * m * labels, bytes_accessed=2 * n * m, transcendentals=0
        ),
        name="gradient",
    )(resid, stored, *earlier)


def prepare_kernel(
    last, ranks, inverse, left_t, right_t, rates, proj, step, side, suffix_proj, transfer, acc
):
    i = pl.program_id(0)
    eye = lax.broadcasted_iota(jnp.int32, (R, R), 0) == lax.broadcasted_iota(jnp.int32, (R, R), 1)

    @pl.when(i == 0)
    def _():
        acc[...] = eye.astype(f32)

    kept = lax.broadcasted_iota(jnp.int32, (R, B), 0) < ranks[last - i]
    left = jnp.where(kept, left_t[0].astype(f32), 0.0).astype(bf16)
    right = jnp.where(kept, right_t[0].astype(f32), 0.0).astype(bf16)
    high, low = split(inverse[0])
    p = dot(right, high, 1, 0) + dot(right, low, 1, 0)
    proj[...] = p
    side[...] = dot(left, high, 1, 1) + dot(left, low, 1, 1)
    ph, plow = split(p)
    decay = jnp.exp(rates[0] * (-1.0 / NB))
    a = jnp.where(eye, decay, 0.0) - (dot(ph, left, 1, 1) + dot(plow, left, 1, 1))
    step[0] = a
    suffix = acc[...]
    suffix_proj[...] = dot3(suffix, p, 1, 0)
    suffix = jnp.dot(suffix, a, precision=highest, preferred_element_type=f32)
    acc[...] = suffix
    transfer[...] = suffix


def prepare(block_ranks, diag_inv, left_t, right_t, rates):
    count = diag_inv.shape[0]
    last = count - 1
    back = lambda i, ranks: (last - i, 0, 0)
    wide = lambda i, ranks: (0, last - i)
    wide_shape = jax.ShapeDtypeStruct((R, count * B), f32)
    return pl.pallas_call(
        functools.partial(prepare_kernel, last),
        grid_spec=pltpu.PrefetchScalarGridSpec(
            num_scalar_prefetch=1,
            grid=(count,),
            in_specs=[
                pl.BlockSpec((1, B, B), back),
                pl.BlockSpec((1, R, B), back),
                pl.BlockSpec((1, R, B), back),
                pl.BlockSpec((1, 1, R), back),
            ],
            out_specs=[
                pl.BlockSpec((R, B), wide),
                pl.BlockSpec((1, R, R), back),
                pl.BlockSpec((R, B), wide),
                pl.BlockSpec((R, B), wide),
                pl.BlockSpec((R, R), lambda i, ranks: (0, 0)),
            ],
            scratch_shapes=[pltpu.VMEM((R, R), f32)],
        ),
        out_shape=[
            wide_shape,
            jax.ShapeDtypeStruct((count, R, R), f32),
            wide_shape,
            wide_shape,
            jax.ShapeDtypeStruct((R, R), f32),
        ],
        cost_estimate=pl.CostEstimate(
            flops=8 * count * R * B * B, bytes_accessed=6 * count * B * B, transcendentals=0
        ),
        compiler_params=pltpu.CompilerParams(vmem_limit_bytes=24 << 20),
        name="prepare",
    )(block_ranks, diag_inv, left_t, right_t, rates[:, None, :])


def prefix_kernel(step, side, out):
    moved = None
    for k in range(step.shape[0]):
        cols = slice(k * B, (k + 1) * B)
        if moved is None:
            out[:, cols] = side[:, cols]
            moved = step[k].T
        else:
            out[:, cols] = dot3(moved, side[:, cols], 1, 0)
            if k + 1 < step.shape[0]:
                moved = dot3(moved, step[k], 1, 1)


def prefix_side(step, side):
    return pl.pallas_call(
        prefix_kernel,
        out_shape=jax.ShapeDtypeStruct(side.shape, f32),
        cost_estimate=pl.CostEstimate(
            flops=6 * R * side.size, bytes_accessed=8 * side.size, transcendentals=0
        ),
        compiler_params=pltpu.CompilerParams(vmem_limit_bytes=40 << 20),
        name="prefix",
    )(step, side)


def offset_kernel(grad, suffix_proj, transfer, out):
    found = dot3(grad[...], suffix_proj[...], 1, 1)
    high = found.astype(bf16).astype(f32)
    t = transfer[...]
    rows = jnp.concatenate(
        [
            jnp.concatenate([t[: R // 2], t[R // 2 :]], axis=1),
            jnp.concatenate([high, found - high], axis=1),
            jnp.zeros((8, 2 * R), f32),
        ]
    ).astype(bf16)
    for e in range(out.shape[0]):
        out[e] = rows


def offset_messages(grad, suffix_proj, transfer, count):
    return pl.pallas_call(
        offset_kernel,
        out_shape=pltpu.HBM((count, R // 2 + 16, 2 * R), bf16),
        compiler_params=pltpu.CompilerParams(vmem_limit_bytes=40 << 20),
        name="offset",
    )(grad, suffix_proj, transfer)


def local_kernel(grad, inverse, proj, step, side, solved, state):
    @pl.when(pl.program_id(0) == 0)
    def _():
        state[...] = jnp.zeros_like(state)

    g = grad[...]
    gh = g.astype(bf16).astype(f32)
    pair = jnp.concatenate([gh, g - gh]).astype(bf16)
    n = g.shape[0]

    def times(matrix):
        high, low = split(matrix)
        main = dot(pair, high, 1, 1)
        return (main[:n] + main[n:]) + dot(pair, low, 1, 1)[:n]

    entered = state[...]
    solved[...] = times(inverse[0]) - dot3(entered, side[...], 1, 0)
    state[...] = dot3(entered, step[0], 1, 1) + times(proj[...])


def local_solve(grad, diag_inv, proj, step, side):
    count = diag_inv.shape[0]
    labels = grad.shape[0]
    return pl.pallas_call(
        local_kernel,
        grid=(count,),
        in_specs=[
            pl.BlockSpec((labels, B), lambda i: (0, i)),
            pl.BlockSpec((1, B, B), lambda i: (i, 0, 0)),
            pl.BlockSpec((R, B), lambda i: (0, i)),
            pl.BlockSpec((1, R, R), lambda i: (i, 0, 0)),
            pl.BlockSpec((R, B), lambda i: (0, i)),
        ],
        out_specs=pl.BlockSpec((labels, B), lambda i: (0, i)),
        out_shape=jax.ShapeDtypeStruct((labels, count * B), f32),
        scratch_shapes=[pltpu.VMEM((labels, R), f32)],
        cost_estimate=pl.CostEstimate(
            flops=6 * count * labels * B * B, bytes_accessed=4 * count * B * B, transcendentals=0
        ),
        compiler_params=pltpu.CompilerParams(vmem_limit_bytes=40 << 20),
        name="local_solve",
    )(grad, diag_inv, proj, step, side)


def finish_kernel(place, messages, solved, side, out):
    mine = place[0]
    count = messages.shape[0]
    half = R // 2

    def read(e):
        got = messages[e].astype(f32)
        transfer = jnp.concatenate([got[:half, :R], got[:half, R:]]).astype(bf16)
        rows = got[half : half + 8]
        return transfer, rows[:, :R] + rows[:, R:]

    def apply(rows, transfer):
        high, low = split(rows)
        return dot(high, transfer, 1, 1) + dot(low, transfer, 1, 1)

    eye = lax.broadcasted_iota(jnp.int32, (R, R), 0) == lax.broadcasted_iota(jnp.int32, (R, R), 1)
    early = jnp.zeros((8, R), f32)
    late = jnp.concatenate([early, eye.astype(f32)])
    blank = jnp.zeros((R, R), f32)
    for e in range(count // 2):
        transfer, rows = read(e)
        early = jnp.where(e < mine, apply(early, transfer) + rows, early)
        f = e + count // 2
        transfer, rows = read(f)
        moved = apply(late, transfer) + jnp.concatenate([rows, blank])
        late = jnp.where(f < mine, moved, late)
    entering = late[:8] + dot3(early, late[8:], 1, 0)
    z = solved[...] - dot3(entering, side[...], 1, 0)
    top = jnp.max(jnp.abs(z), axis=1, keepdims=True)
    power = jnp.ceil(jnp.log2(jnp.maximum(top, 1e-30)))
    width = z.shape[1]
    out[:, :width] = z * jnp.exp2(-power)
    out[:, width:] = jnp.broadcast_to(power, (8, 2 * R))


def finish(place, messages, solved, side):
    labels, m = solved.shape
    return pl.pallas_call(
        finish_kernel,
        grid_spec=pltpu.PrefetchScalarGridSpec(
            num_scalar_prefetch=1,
            grid=(),
            in_specs=[vmem, vmem, vmem],
            out_specs=vmem,
        ),
        out_shape=jax.ShapeDtypeStruct((labels, m + 2 * R), f32),
        compiler_params=pltpu.CompilerParams(vmem_limit_bytes=40 << 20),
        name="finish",
    )(place.reshape(1), messages, solved, side)


def unscaled_kernel(powers, scaled, out):
    out[...] = (scaled[...] * jnp.exp2(powers[:, :1])).T


def unscaled(whole, cols=1024):
    labels = whole.shape[0]
    m = whole.shape[1] - 2 * R
    return pl.pallas_call(
        unscaled_kernel,
        grid=(m // cols,),
        in_specs=[
            pl.BlockSpec((labels, 2 * R), lambda i: (0, m // (2 * R))),
            pl.BlockSpec((labels, cols), lambda i: (0, i)),
        ],
        out_specs=pl.BlockSpec((cols, labels), lambda i: (i, 0)),
        out_shape=jax.ShapeDtypeStruct((m, labels), f32),
        compiler_params=pltpu.CompilerParams(vmem_limit_bytes=40 << 20),
        name="unscaled",
    )(whole, whole)


def sent_to_all(array, axis):
    copies = jnp.broadcast_to(array, (lax.axis_size(axis), *array.shape))
    return lax.all_to_all(copies, axis, split_axis=0, concat_axis=0, tiled=True)


def to_partner(array):
    return lax.ppermute(array, "c", [(0, 1), (1, 0)])


def body(points, centers, coeffs, targets, diag_inv, low_left, low_right, decay_rates, block_ranks):
    n, labels = targets.shape
    m = centers.shape[0]
    chips, samp = lax.axis_size("z"), lax.axis_size("samp")
    chip, core = lax.axis_index("z"), lax.axis_index("c")
    place = chip * 2 + core
    share = n // (2 * chips)

    in_hbm = lambda array: pltpu.with_memory_space_constraint(array, pltpu.HBM)
    points, share_at, place = lax.optimization_barrier((points, core * chips + chip, place))
    diag_inv, points_t, centers_t = in_hbm(diag_inv), in_hbm(points.T), in_hbm(centers.T)
    stored_b, pred_b, extended, coeffs_v = predict(
        1 - core, points_t, centers_t, in_hbm(coeffs), True
    )
    from_partner = to_partner(pred_b)
    stored_a, pred_a = predict(core, points_t, extended, coeffs_v, False)
    pair_sum = (pred_a + from_partner).astype(wire).reshape(chips, share, labels)
    arrived = lax.all_to_all(pair_sum, "z", 0, 0, tiled=True)
    pred_own = arrived.astype(f32).sum(axis=0)
    resid = residual_copies(share_at, pred_own, in_hbm(targets), chips)
    resid_a = lax.all_to_all(resid, "z", 0, 0, tiled=True).reshape(n // 2, labels)
    resid_b = to_partner(resid_a)

    partial = gradient_t(resid_a, stored_a)
    partial = gradient_t(resid_b, stored_b, partial)
    own = labels // samp
    sent = partial.astype(wire).reshape(samp, own, m)
    sent, block_ranks = lax.optimization_barrier((sent, block_ranks))
    arrived = lax.all_to_all(sent, "samp", 0, 0, tiled=True)
    prepared = prepare(
        block_ranks,
        diag_inv,
        jnp.swapaxes(low_left, 1, 2),
        jnp.swapaxes(low_right, 1, 2),
        decay_rates,
    )
    side_prefix = prefix_side(prepared[1], prepared[2])
    arrived, prepared, side_prefix = lax.optimization_barrier((arrived, prepared, side_prefix))
    proj, step, side, suffix_proj, transfer = prepared
    own_coeffs = lax.dynamic_slice_in_dim(coeffs, lax.axis_index("samp") * own, own, 1).T
    scaling = 1.0 / math.sqrt(n * samp)
    grad = arrived.astype(f32).sum(axis=0) * scaling + ridge_weight * own_coeffs.astype(f32)

    messages = offset_messages(grad, suffix_proj, in_hbm(transfer), 2 * chips)
    messages = lax.all_to_all(messages, ("z", "c"), 0, 0, tiled=True)
    solved = local_solve(grad, diag_inv, proj, step, side)
    direction = finish(place, messages, solved, side_prefix)
    whole = sent_to_all(direction.astype(wire), "samp").reshape(labels, m + 2 * R)
    return unscaled(whole.astype(f32))


def solution(mesh):
    finer = Mesh(mesh.devices.reshape(mesh.shape["samp"], -1, 2), ("samp", "z", "c"))
    ind = ("z", "c")
    placed = (
        P("samp", None),
        P(ind, None),
        P(ind, None),
        P("samp", None),
        P(ind, None, None),
        P(ind, None, None),
        P(ind, None, None),
        P(ind, None),
        P(ind),
    )
    return jax.shard_map(
        body, mesh=finer, in_specs=placed, out_specs=P(ind, None), check_vma=False
    )
```
